256 devices in a mesh: fold: 8 (over x, core), dom: 32 (over z, y).
Axes of the slice: x: 4, y: 4, z: 8, core: 2. Of those that a mesh axis runs over, the one named last changes fastest.
Arguments:
- iterate: float32 [176, 8, 65536], P(None, 'fold', 'dom'), may hold values from -6 to 6
- right_side: float32 [176, 8, 65536], P(None, 'fold', 'dom'), may hold values from -6 to 6
- jacobian: float32 [8, 65536], P('fold', 'dom'), may hold values from 0.5 to 2
- face_scale: float32 [4, 8, 65536], P(None, 'fold', 'dom'), may hold values from 0.3 to 1.5
- face_offset: int32 [4, 8, 65536], P(None, 'fold', 'dom'), may hold values from -512 to 512, as said below
- agglomerate: int32 [8, 65536], P('fold', 'dom'), may hold values from 0 to 255, as said below
- live_count: int32 [8, 32], P('fold', 'dom'), may hold values from 819 to 2048, as said below
- stiff_fine: float32 [176, 176], replicated, as said below
- flux_fine: float32 [4, 176, 176], replicated, may hold values from -0.4375 to 0.4375
- smoother: float32 [176, 176], replicated
- restrict_mid: float32 [56, 176], replicated, may hold values from -0.4375 to 0.4375
- restrict_low: float32 [24, 56], replicated, may hold values from -0.75 to 0.75
Outputs:
- updated: float32 [176, 8, 65536], P(None, 'fold', 'dom')
- residual: float32 [176, 8, 65536], P(None, 'fold', 'dom')
The draws below stay inside these ranges and needn't reach their ends.
Inputs may be any that keep to these rules, and one draw needn't show every extreme that they name: `face_offset`: 0 marks a wall face; an offset that leads outside its fold plane also acts as a wall; offsets of +512 and -512 occur. `agglomerate`: coarse slots are local to the device of the element. `live_count`: the elements of a device fill its first slots; some device is full. `stiff_fine`: symmetric.
All inputs are finite; a program needn't handle non-finite values.
Results may differ from the reference program's by a relative error of at most 0.0003.
Values sent between devices are 32-bit elements; how exact they have to be, the bound alone decides.
A program may use at most 128 MiB of HBM per device.

```python
import math
from functools import partial
import jax
import jax.numpy as jnp
from jax import lax

NP0 = 176
NP1 = 56
NP2 = 24
FACES = 4
AGG = 8
HLEV = 2
E_DEV = 2048
HALO = 512
EC_DEV = 256
ED = 65536
N_FOLD = 8
N_DOM = 32


def draw_live_count(key, part):
    first_key, second_key = jax.random.split(key)
    spread = jax.random.randint(first_key, (N_FOLD * N_DOM,), 0, 61)
    counts = E_DEV * (40 + spread) // 100
    chosen = jax.random.randint(second_key, (), 0, N_FOLD * N_DOM)
    counts = jnp.where(jnp.arange(N_FOLD * N_DOM) == chosen, E_DEV, counts)
    return counts.reshape(N_FOLD, N_DOM).astype(jnp.int32)


def draw_face_offset(key, part):
    size_key, sign_key, wall_key = jax.random.split(key, 3)
    shape = (FACES, N_FOLD, ED)
    magnitude = jax.random.randint(size_key, shape, 1, HALO + 1)
    signs = 2 * jax.random.randint(sign_key, shape, 0, 2) - 1
    walls = jax.random.randint(wall_key, shape, 0, 8) == 0
    offsets = jnp.where(walls, 0, magnitude * signs)
    offsets = offsets.at[0, :, 0].set(HALO)
    offsets = offsets.at[1, :, ED - 1].set(-HALO)
    return offsets.astype(jnp.int32)


def draw_agglomerate(key, part):
    jitter = jax.random.randint(key, (N_FOLD, ED), -(AGG // 2), AGG // 2 + 1)
    local = jnp.arange(ED, dtype=jnp.int32) % E_DEV
    return jnp.clip((local[None, :] + jitter) // AGG, 0, E_DEV // AGG - 1).astype(jnp.int32)


def draw_stiff_fine(key, part):
    noise = jax.random.normal(key, (NP0, NP0), jnp.float32)
    return 3.0 * jnp.eye(NP0, dtype=jnp.float32) + (noise + noise.T) * (0.9 / jnp.sqrt(2.0 * NP0))


def draw_smoother(key, part):
    noise = jax.random.normal(key, (NP0, NP0), jnp.float32)
    return jnp.eye(NP0, dtype=jnp.float32) / 3.0 + noise * (0.3 / jnp.sqrt(1.0 * NP0))


def shard_levels(rng, shape, shards, smallest, high):
    loudness, own = 1.0, jax.random.fold_in(rng, 6)
    for position, blocks in shards:
        draws = jnp.exp(jax.random.uniform(jax.random.fold_in(own, position), (blocks,), jnp.float32, smallest / len(shards), high / len(shards)))
        loudness = loudness * jnp.repeat(draws, shape[position] // blocks).reshape([-1 if axis == position else 1 for axis in range(len(shape))])
    return loudness


def scatter_about(stream_key, shape, scale, most, cuts=(), kind=jnp.bfloat16):
    drawn = jax.random.normal(stream_key, shape, jnp.float32) * scale
    if len(cuts) > 0:
        drawn = shard_levels(stream_key, shape, cuts, -0.22, 0.18) * drawn
    return jnp.clip(drawn, min=-most, max=most).astype(kind)


def setup_inputs(seed: int = 0) -> dict:
    streams_of = jax.random.split(jax.random.key(seed), 13)
    iterate = scatter_about(streams_of[0], (NP0, N_FOLD, ED), 1.0, 6.0, ((1, 8), (2, 32)), jnp.float32)
    right_side = scatter_about(streams_of[1], (NP0, N_FOLD, ED), 1.0, 6.0, ((1, 8), (2, 32)), jnp.float32)
    jacobian = jnp.clip(jnp.exp(math.log(2.0) - 1.3862944 * jax.random.uniform(streams_of[2], (N_FOLD, ED), jnp.float32) ** shard_levels(streams_of[2], (N_FOLD, ED), ((0, 8), (1, 32)), -0.2, 0.2)), 0.5, 2.0)
    face_scale = jnp.clip(jnp.exp(math.log(1.5) - 1.60943787 * jax.random.uniform(streams_of[3], (FACES, N_FOLD, ED), jnp.float32) ** shard_levels(streams_of[3], (FACES, N_FOLD, ED), ((1, 8), (2, 32)), -0.2, 0.2)), 0.3, 1.5)
    face_offset = draw_face_offset(jax.random.fold_in(streams_of[12], 71), 0)
    agglomerate = draw_agglomerate(jax.random.fold_in(streams_of[12], 71), 0)
    live_count = draw_live_count(jax.random.fold_in(streams_of[12], 71), 0)
    stiff_fine = draw_stiff_fine(jax.random.fold_in(streams_of[12], 71), 0)
    flux_fine = scatter_about(streams_of[8], (FACES, NP0, NP0), NP0 ** -0.5, 0.4375, (), jnp.float32)
    smoother = draw_smoother(jax.random.fold_in(streams_of[12], 71), 0)
    restrict_mid = scatter_about(streams_of[10], (NP1, NP0), NP0 ** -0.5, 0.4375, (), jnp.float32)
    restrict_low = scatter_about(streams_of[11], (NP2, NP1), NP1 ** -0.5, 0.75, (), jnp.float32)
    return {"iterate": iterate, "right_side": right_side, "jacobian": jacobian, "face_scale": face_scale, "face_offset": face_offset, "agglomerate": agglomerate, "live_count": live_count, "stiff_fine": stiff_fine, "flux_fine": flux_fine, "smoother": smoother, "restrict_mid": restrict_mid, "restrict_low": restrict_low}


PRECISE = lax.Precision.HIGHEST
DAMPING = 0.8


def product(former, latter):
    return jnp.dot(former, latter, precision=PRECISE, preferred_element_type=jnp.float32)


def galerkin(restrict, matrix):
    return product(product(restrict, matrix), restrict.T)


def galerkin_all(restrict, fluxes):
    return jax.vmap(partial(galerkin, restrict))(fluxes)


def plane_apply(vector, jac_row, scale_rows, offset_rows, active, stiffness, fluxes):
    columns = vector.shape[1]
    padded = jnp.pad(vector, ((0, 0), (HALO, HALO)))
    target = jnp.arange(columns, dtype=jnp.int32)[None, :] + offset_rows
    inside = (offset_rows != 0) & (target >= 0) & (target < columns)
    picked = jnp.take(padded, (target + HALO).astype(jnp.int32), axis=1)
    weights = jnp.where(inside, scale_rows, jnp.zeros_like(scale_rows))
    coupled = jnp.einsum("fab,bfn->an", fluxes, picked * weights[None], precision=PRECISE)
    return active * (jac_row * product(stiffness, vector) + coupled)


def plane_active(live_row):
    columns = jnp.arange(ED, dtype=jnp.int32)
    owner = (columns // E_DEV).astype(jnp.int32)
    return ((columns % E_DEV) < jnp.take(live_row, owner)).astype(jnp.float32)[None, :]


def coarse_chain(coarse, stiff_low, diag_low):
    sections = []
    for height in range(HLEV):
        factor = AGG * 2 ** height
        sections.append(DAMPING * coarse / (factor * diag_low))
        residue = coarse - DAMPING * jnp.einsum("ab,gbx->gax", stiff_low, coarse / diag_low, precision=PRECISE)
        groups = residue.shape[0]
        coarse = residue.reshape(groups // 2, 2, residue.shape[1], residue.shape[2]).sum(axis=1)
    result = DAMPING * coarse / (AGG * 2 ** HLEV * diag_low)
    for height in reversed(range(HLEV)):
        result = sections[height] + jnp.repeat(result, 2, axis=0)
    return result


def planes_first(array):
    return jnp.moveaxis(array, 1, 0)


def reference(iterate, right_side, jacobian, face_scale, face_offset, agglomerate, live_count, stiff_fine, flux_fine, smoother, restrict_mid, restrict_low):
    stiff_mid = galerkin(restrict_mid, stiff_fine)
    flux_mid = galerkin_all(restrict_mid, flux_fine)
    stiff_low = galerkin(restrict_low, stiff_mid)
    flux_low = galerkin_all(restrict_low, flux_mid)
    diag_mid = jnp.diagonal(stiff_mid)[:, None]
    diag_low = jnp.diagonal(stiff_low)[:, None]
    coarse_index = (jnp.arange(ED, dtype=jnp.int32) // E_DEV).astype(jnp.int32) * EC_DEV

    def descend(planes):
        vec_iter, vec_rhs, jac_line, scale_rows, offset_rows, agg_row, live_row = planes
        jac_row = jac_line[None, :]
        active = plane_active(live_row)
        masked = active * vec_iter
        target_side = active * vec_rhs
        first_res = target_side - plane_apply(masked, jac_row, scale_rows, offset_rows, active, stiff_fine, flux_fine)
        smoothed = masked + active * product(smoother, first_res) / jac_row
        second = target_side - plane_apply(smoothed, jac_row, scale_rows, offset_rows, active, stiff_fine, flux_fine)
        mid_rhs = product(restrict_mid, second)
        mid_corr = DAMPING * active * mid_rhs / (jac_row * diag_mid)
        mid_res = mid_rhs - plane_apply(mid_corr, jac_row, scale_rows, offset_rows, active, stiff_mid, flux_mid)
        low_rhs = product(restrict_low, mid_res)
        low_corr = DAMPING * active * low_rhs / (jac_row * diag_low)
        low_res = low_rhs - plane_apply(low_corr, jac_row, scale_rows, offset_rows, active, stiff_low, flux_low)
        coarse_id = (coarse_index + agg_row).astype(jnp.int32)
        coarse = jax.ops.segment_sum(low_res.T, coarse_id, num_segments=EC_DEV * N_DOM).T
        return smoothed, mid_corr, low_corr, coarse

    smoothed_all, mid_all, low_all, coarse_all = lax.map(descend, (planes_first(iterate), planes_first(right_side), jacobian, planes_first(face_scale), planes_first(face_offset), agglomerate, live_count))
    corr_all = coarse_chain(coarse_all, stiff_low, diag_low)

    def ascend(planes):
        smoothed, mid_corr, low_corr, coarse_corr, vec_rhs, jac_line, scale_rows, offset_rows, agg_row, live_row = planes
        jac_row = jac_line[None, :]
        active = plane_active(live_row)
        coarse_id = (coarse_index + agg_row).astype(jnp.int32)
        low_total = low_corr + active * jnp.take(coarse_corr, coarse_id, axis=1)
        mid_total = mid_corr + product(restrict_low.T, low_total)
        updated = smoothed + product(restrict_mid.T, mid_total)
        residual = active * vec_rhs - plane_apply(updated, jac_row, scale_rows, offset_rows, active, stiff_fine, flux_fine)
        return updated, residual

    updated_all, residual_all = lax.map(ascend, (smoothed_all, mid_all, low_all, corr_all, planes_first(right_side), jacobian, planes_first(face_scale), planes_first(face_offset), agglomerate, live_count))
    return planes_first(updated_all), planes_first(residual_all)
```

```python
from functools import partial

import jax
import jax.numpy as jnp
from jax import lax
from jax.experimental import pallas as pl
from jax.experimental.pallas import tpu as pltpu
from jax.sharding import PartitionSpec as P

NP0, NP1, NP2 = 176, 56, 24
FACES = 4
AGG = 8
HLEV = 2
HALO = 512
EC_DEV = 256
E_DEV = 2048
LANES = 128
PAIR = 256
PAIRS = E_DEV // PAIR
SIDE = HALO // PAIR
SPAN = 2 * SIDE + 1
EXT = PAIRS + 2 * SIDE
ROWS_PER = E_DEV // LANES
DAMPING = 0.8
KF = 896
KM = 288
KL = 128
NPM = 64
NPL = 32
MESH = pl.DeviceIdType.MESH
F32, BF16 = jnp.float32, jnp.bfloat16
NN = (((1,), (0,)), ((), ()))
NT = (((1,), (1,)), ((), ()))


def exact(a, b, dims=NN):
    return lax.dot_general(a, b, dims, precision=lax.Precision.HIGHEST, preferred_element_type=F32)


def parts(x):
    high = x.astype(BF16)
    low = (x - high.astype(F32)).astype(BF16)
    return high, low


def store_parts(ref, x, rows):
    high, low = parts(x)
    ref[pl.ds(0, x.shape[0]), :] = high
    ref[pl.ds(rows, x.shape[0]), :] = low


def product(split_ref, rows, high, low):
    both = jnp.dot(split_ref[...], high, preferred_element_type=F32)
    rest = jnp.dot(split_ref[pl.ds(0, rows), :], low, preferred_element_type=F32)
    return both[:rows] + both[rows:] + rest


def kernel(
    n_dom,
    n_fold,
    iter_ref,
    rhs_ref,
    jac_ref,
    scale_ref,
    offset_ref,
    agg_ref,
    live_ref,
    stiff_ref,
    flux_ref,
    smoother_ref,
    rmid_ref,
    rlow_ref,
    upd_ref,
    res_ref,
    e1,
    e2,
    e3,
    e4,
    e5,
    split1,
    split2,
    pick,
    second,
    mid_rhs,
    low_rhs,
    low_res,
    feed_high,
    feed_low,
    fine_f32,
    fine_split,
    smooth_split,
    rmid_split,
    mid_f32,
    mid_split,
    lift_f32,
    lift_split,
    low_f32,
    low_split,
    rmid_t_split,
    swap_out,
    swap_in,
    send_sem,
    recv_sem,
    swap_send,
    swap_recv,
):
    me = lax.axis_index("dom")
    fold = lax.axis_index("fold")
    right = lax.rem(me + 1, n_dom)
    left = lax.rem(me + n_dom - 1, n_dom)
    partners = []
    for height in range(HLEV):
        step = 2**height
        bit = (fold // step) % 2
        partners.append(fold + step - 2 * step * bit)

    barrier = pltpu.get_barrier_semaphore()
    for other in (left, right):
        pl.semaphore_signal(barrier, inc=1, device_id={"dom": other}, device_id_type=MESH)
    for other in partners:
        pl.semaphore_signal(barrier, inc=1, device_id={"fold": other}, device_id_type=MESH)

    lane = lax.broadcasted_iota(jnp.int32, (1, PAIR), 1)
    live = live_ref[0, 0]

    def row_of(ref, base, u):
        return jnp.concatenate(
            [ref[pl.ds(base + 2 * u, 1), :], ref[pl.ds(base + 2 * u + 1, 1), :]], axis=1
        )

    def active_of(u):
        return jnp.where(u * PAIR + lane < live, 1.0, 0.0).astype(F32)

    def jac_of(u):
        return row_of(jac_ref, 0, u)

    def weight_of(f, u):
        offset = row_of(offset_ref, f * ROWS_PER, u)
        target = me * E_DEV + u * PAIR + lane + offset
        inside = (offset != 0) & (target >= 0) & (target < n_dom * E_DEV)
        return jnp.where(inside, row_of(scale_ref, f * ROWS_PER, u), 0.0)

    def wide(ref, u):
        return jnp.concatenate(
            [ref[pl.ds(2 * u + h, NP0, stride=ROWS_PER), :] for h in range(2)], axis=1
        )

    def put_wide(ref, u, value):
        for h in range(2):
            ref[pl.ds(2 * u + h, NP0, stride=ROWS_PER), :] = value[:, h * LANES : (h + 1) * LANES]

    def exchange(k, buffer):
        to_right = pltpu.make_async_remote_copy(
            src_ref=buffer.at[pl.ds(PAIRS, SIDE)],
            dst_ref=buffer.at[pl.ds(0, SIDE)],
            send_sem=send_sem.at[k, 0],
            recv_sem=recv_sem.at[k, 0],
            device_id={"dom": right},
            device_id_type=MESH,
        )
        to_left = pltpu.make_async_remote_copy(
            src_ref=buffer.at[pl.ds(SIDE, SIDE)],
            dst_ref=buffer.at[pl.ds(SIDE + PAIRS, SIDE)],
            send_sem=send_sem.at[k, 1],
            recv_sem=recv_sem.at[k, 1],
            device_id={"dom": left},
            device_id_type=MESH,
        )
        to_right.start()
        to_left.start()
        return to_right, to_left

    def finish(copies):
        for copy in copies:
            copy.wait()

    def over(first, last, body):
        lax.fori_loop(first, last, lambda i, c: (body(i), c)[1], 0)

    def over_edges(body):
        lax.fori_loop(
            0, 2 * SIDE, lambda i, c: (body(i + (i // SIDE) * (PAIRS - 2 * SIDE)), c)[1], 0
        )

    def mask_block(u):
        e1[u + SIDE] = active_of(u) * wide(iter_ref, u)

    over(0, PAIRS, mask_block)
    pl.semaphore_wait(barrier, 2 + HLEV)
    first_halo = exchange(0, e1)

    def split_block(source, target, b):
        store_parts(target.at[b], source[b], NP0)

    def split_halo(source, target):
        for b in (*range(SIDE), *range(SIDE + PAIRS, EXT)):
            split_block(source, target, b)

    over(SIDE, SIDE + PAIRS, lambda b: split_block(e1, split1, b))

    fine_f32[...] = jnp.zeros_like(fine_f32)
    for f in range(FACES):
        fine_f32[:, f * NP0 : (f + 1) * NP0] = flux_ref[f]
    fine_f32[:, FACES * NP0 : (FACES + 1) * NP0] = stiff_ref[...]
    store_parts(fine_split, fine_f32[...], NP0)
    store_parts(smooth_split, smoother_ref[...], NP0)
    feed_high[...] = jnp.zeros_like(feed_high)
    feed_low[...] = jnp.zeros_like(feed_low)

    def build_pick(u, f):
        reach = lane + row_of(offset_ref, f * ROWS_PER, u) + HALO
        rows = lax.broadcasted_iota(jnp.int32, (PAIR, PAIR), 0)
        for j in range(SPAN):
            pick[u, f, pl.ds(j * PAIR, PAIR), :] = jnp.where(
                rows + j * PAIR == reach, 1.0, 0.0
            ).astype(BF16)

    def fine_apply(u, source, split, build):
        around = jnp.concatenate([split[u + j] for j in range(SPAN)], axis=1)
        for f in range(FACES):
            if build:
                build_pick(u, f)
            both = jnp.dot(around, pick[u, f], preferred_element_type=F32)
            high, low = parts((both[:NP0] + both[NP0:]) * weight_of(f, u))
            feed_high[pl.ds(f * NP0, NP0), :] = high
            feed_low[pl.ds(f * NP0, NP0), :] = low
        high, low = parts(jac_of(u) * source[u + SIDE])
        feed_high[pl.ds(FACES * NP0, NP0), :] = high
        feed_low[pl.ds(FACES * NP0, NP0), :] = low
        return product(fine_split, NP0, feed_high[...], feed_low[...])

    def smooth_block(u):
        active = active_of(u)
        first_res = active * (wide(rhs_ref, u) - fine_apply(u, e1, split1, True))
        high, low = parts(first_res)
        update = product(smooth_split, NP0, high, low)
        block = e1[u + SIDE] + update * (active / jac_of(u))
        e2[u + SIDE] = block
        store_parts(split2.at[u + SIDE], block, NP0)

    over(SIDE, PAIRS - SIDE, smooth_block)
    finish(first_halo)
    split_halo(e1, split1)
    over_edges(smooth_block)
    second_halo = exchange(1, e2)

    rmid = rmid_ref[...]
    rlow = rlow_ref[...]
    mid_f32[...] = jnp.zeros_like(mid_f32)
    lift_f32[...] = jnp.zeros_like(lift_f32)
    low_f32[...] = jnp.zeros_like(low_f32)
    rmid_split[...] = jnp.zeros_like(rmid_split)
    store_parts(rmid_split, rmid, NPM)

    def identity(n):
        rows = lax.broadcasted_iota(jnp.int32, (n, n), 0)
        cols = lax.broadcasted_iota(jnp.int32, (n, n), 1)
        return jnp.where(rows == cols, 1.0, 0.0).astype(F32)

    for f in range(FACES + 1):
        matrix = flux_ref[f] if f < FACES else stiff_ref[...]
        mid_matrix = exact(exact(rmid, matrix), rmid, NT)
        mid_f32[0:NP1, f * NP1 : (f + 1) * NP1] = mid_matrix
        lift_f32[:, f * NP1 : (f + 1) * NP1] = exact(matrix, rmid, NT)
        low_matrix = exact(exact(rlow, mid_matrix), rlow, NT)
        low_f32[0:NP2, f * NP2 : (f + 1) * NP2] = low_matrix
    stiff_low = low_matrix
    diag_mid = jnp.sum(mid_matrix * identity(NP1), axis=1, keepdims=True)
    diag_low = jnp.sum(low_matrix * identity(NP2), axis=1, keepdims=True)
    store_parts(mid_split, mid_f32[...], NPM)
    store_parts(lift_split, lift_f32[...], NP0)
    store_parts(low_split, low_f32[...], NPL)
    rmid_t_split[...] = jnp.zeros_like(rmid_t_split)
    rmid_t_high, rmid_t_low = parts(exact(identity(NP0), rmid, NT))
    rmid_t_split[pl.ds(0, NP0), 0:NP1] = rmid_t_high
    rmid_t_split[pl.ds(NP0, NP0), 0:NP1] = rmid_t_low
    rlow_t = exact(identity(NP1), rlow, NT)

    def second_block(u):
        active = active_of(u)
        block = active * (wide(rhs_ref, u) - fine_apply(u, e2, split2, False))
        second[u] = block
        high, low = parts(block)
        rhs = product(rmid_split, NPM, high, low)[:NP1]
        mid_rhs[u] = rhs
        e3[u + SIDE] = rhs * (DAMPING * active / jac_of(u)) / diag_mid

    over(SIDE, PAIRS - SIDE, second_block)
    finish(second_halo)
    split_halo(e2, split2)
    over_edges(second_block)
    mid_halo = exchange(2, e3)

    def gathered(u, buffer, rows, padding):
        reach_lane = lax.broadcasted_iota(jnp.int32, (8, LANES), 1)
        pieces = []
        for f in range(FACES):
            halves = []
            for h in range(2):
                offset = offset_ref[pl.ds(f * ROWS_PER + 2 * u + h, 1), :]
                reach = jnp.broadcast_to(offset, (8, LANES)) + reach_lane + HALO
                inner = reach & (LANES - 1)
                outer = reach >> 7
                groups = []
                for g in range(rows // 8):
                    value = jnp.zeros((8, LANES), F32)
                    for j in range(2 * HALO // LANES + 1):
                        b = h + j
                        source = buffer[
                            u + b // 2, pl.ds(8 * g, 8), pl.ds((b % 2) * LANES, LANES)
                        ]
                        found = jnp.take_along_axis(source, inner, axis=1)
                        value = jnp.where(outer == j, found, value)
                    groups.append(value)
                halves.append(jnp.concatenate(groups, axis=0))
            pieces.append(jnp.concatenate(halves, axis=1) * weight_of(f, u))
        pieces.append(jac_of(u) * buffer[u + SIDE])
        pieces.append(jnp.zeros((padding, PAIR), F32))
        return parts(jnp.concatenate(pieces, axis=0))

    def mid_block(u):
        active = active_of(u)
        high, low = gathered(u, e3, NP1, KM - 5 * NP1)
        mid_res = mid_rhs[u] - active * product(mid_split, NPM, high, low)[:NP1]
        rhs = exact(rlow, mid_res)
        low_rhs[u] = rhs
        e4[u + SIDE] = rhs * (DAMPING * active / jac_of(u)) / diag_low

    over(SIDE, PAIRS - SIDE, mid_block)
    finish(mid_halo)
    over_edges(mid_block)
    low_halo = exchange(3, e4)

    def low_block(u):
        active = active_of(u)
        high, low = gathered(u, e4, NP2, KL - 5 * NP2)
        low_res[u] = low_rhs[u] - active * product(low_split, NPL, high, low)[:NP2]

    over(SIDE, PAIRS - SIDE, low_block)
    finish(low_halo)
    over_edges(low_block)

    def members(u):
        rows = lax.broadcasted_iota(jnp.int32, (EC_DEV, PAIR), 0)
        return jnp.where(rows == row_of(agg_ref, 0, u), 1.0, 0.0).astype(BF16)

    def coarse_block(u, total):
        high, low = parts(
            jnp.concatenate([low_res[u], jnp.zeros((NPL - NP2, PAIR), F32)], axis=0)
        )
        both = lax.dot_general(
            jnp.concatenate([high, low], axis=0), members(u), NT, preferred_element_type=F32
        )
        return total + both[:NP2] + both[NPL : NPL + NP2]

    coarse = lax.fori_loop(0, PAIRS, coarse_block, jnp.zeros((NP2, EC_DEV), F32))
    sections = []
    for height in range(HLEV):
        scaled = coarse / diag_low
        sections.append(scaled * (DAMPING / (AGG * 2**height)))
        residue = coarse - DAMPING * exact(stiff_low, scaled)
        swap_out[height] = residue
        copy = pltpu.make_async_remote_copy(
            src_ref=swap_out.at[height],
            dst_ref=swap_in.at[height],
            send_sem=swap_send.at[height],
            recv_sem=swap_recv.at[height],
            device_id={"fold": partners[height]},
            device_id_type=MESH,
        )
        copy.start()
        copy.wait()
        coarse = residue + swap_in[height]
    corr = coarse / diag_low * (DAMPING / (AGG * 2**HLEV))
    for height in reversed(range(HLEV)):
        corr = sections[height] + corr
    corr_high, corr_low = parts(jnp.concatenate([corr, jnp.zeros((NPL - NP2, EC_DEV), F32)], axis=0))
    corr_split = jnp.concatenate([corr_high, corr_low], axis=0)

    def ascend_block(u):
        active = active_of(u)
        both = jnp.dot(corr_split, members(u), preferred_element_type=F32)
        low_total = e4[u + SIDE] + active * (both[:NP2] + both[NPL : NPL + NP2])
        e5[u + SIDE] = e3[u + SIDE] + exact(rlow_t, low_total)

    over(0, PAIRS, ascend_block)
    last_halo = exchange(4, e5)

    def update_block(u):
        high, low = parts(
            jnp.concatenate([e5[u + SIDE], jnp.zeros((NPM - NP1, PAIR), F32)], axis=0)
        )
        put_wide(upd_ref, u, e2[u + SIDE] + product(rmid_t_split, NP0, high, low))

    over(0, PAIRS, update_block)

    def residual_block(u):
        high, low = gathered(u, e5, NP1, KM - 5 * NP1)
        put_wide(res_ref, u, second[u] - active_of(u) * product(lift_split, NP0, high, low))

    over(SIDE, PAIRS - SIDE, residual_block)
    finish(last_halo)
    over_edges(residual_block)


def on_device(
    n_dom,
    n_fold,
    iterate,
    right_side,
    jacobian,
    face_scale,
    face_offset,
    agglomerate,
    live_count,
    stiff_fine,
    flux_fine,
    smoother,
    restrict_mid,
    restrict_low,
):
    def flat(array):
        return array.reshape(-1, LANES)

    vmem = pl.BlockSpec(memory_space=pltpu.VMEM)
    smem = pl.BlockSpec(memory_space=pltpu.SMEM)
    out = jax.ShapeDtypeStruct((NP0 * ROWS_PER, LANES), F32)
    updated, residual = pl.pallas_call(
        partial(kernel, n_dom, n_fold),
        out_shape=(out, out),
        in_specs=[vmem] * 6 + [smem] + [vmem] * 5,
        out_specs=(vmem, vmem),
        scratch_shapes=[
            pltpu.VMEM((EXT, NP0, PAIR), F32),
            pltpu.VMEM((EXT, NP0, PAIR), F32),
            pltpu.VMEM((EXT, NP1, PAIR), F32),
            pltpu.VMEM((EXT, NP2, PAIR), F32),
            pltpu.VMEM((EXT, NP1, PAIR), F32),
            pltpu.VMEM((EXT, 2 * NP0, PAIR), BF16),
            pltpu.VMEM((EXT, 2 * NP0, PAIR), BF16),
            pltpu.VMEM((PAIRS, FACES, SPAN * PAIR, PAIR), BF16),
            pltpu.VMEM((PAIRS, NP0, PAIR), F32),
            pltpu.VMEM((PAIRS, NP1, PAIR), F32),
            pltpu.VMEM((PAIRS, NP2, PAIR), F32),
            pltpu.VMEM((PAIRS, NP2, PAIR), F32),
            pltpu.VMEM((KF, PAIR), BF16),
            pltpu.VMEM((KF, PAIR), BF16),
            pltpu.VMEM((NP0, KF), F32),
            pltpu.VMEM((2 * NP0, KF), BF16),
            pltpu.VMEM((2 * NP0, NP0), BF16),
            pltpu.VMEM((2 * NPM, NP0), BF16),
            pltpu.VMEM((NPM, KM), F32),
            pltpu.VMEM((2 * NPM, KM), BF16),
            pltpu.VMEM((NP0, KM), F32),
            pltpu.VMEM((2 * NP0, KM), BF16),
            pltpu.VMEM((NPL, KL), F32),
            pltpu.VMEM((2 * NPL, KL), BF16),
            pltpu.VMEM((2 * NP0, NPM), BF16),
            pltpu.VMEM((HLEV, NP2, EC_DEV), F32),
            pltpu.VMEM((HLEV, NP2, EC_DEV), F32),
            pltpu.SemaphoreType.DMA((5, 2)),
            pltpu.SemaphoreType.DMA((5, 2)),
            pltpu.SemaphoreType.DMA((HLEV,)),
            pltpu.SemaphoreType.DMA((HLEV,)),
        ],
        compiler_params=pltpu.CompilerParams(
            collective_id=0, has_side_effects=True, vmem_limit_bytes=60 * 1024 * 1024
        ),
    )(
        flat(iterate),
        flat(right_side),
        flat(jacobian),
        flat(face_scale),
        flat(face_offset),
        flat(agglomerate),
        live_count,
        stiff_fine,
        flux_fine,
        smoother,
        restrict_mid,
        restrict_low,
    )
    return updated.reshape(iterate.shape), residual.reshape(iterate.shape)


def solution(mesh):
    return jax.shard_map(
        partial(on_device, mesh.shape["dom"], mesh.shape["fold"]),
        mesh=mesh,
        in_specs=(
            P(None, "fold", "dom"),
            P(None, "fold", "dom"),
            P("fold", "dom"),
            P(None, "fold", "dom"),
            P(None, "fold", "dom"),
            P("fold", "dom"),
            P("fold", "dom"),
            P(),
            P(),
            P(),
            P(),
            P(),
        ),
        out_specs=(P(None, "fold", "dom"), P(None, "fold", "dom")),
        check_vma=False,
    )
```

```python
from functools import partial

import jax
import jax.numpy as jnp
from jax import lax
from jax.experimental import pallas as pl
from jax.experimental.pallas import tpu as pltpu
from jax.sharding import PartitionSpec as P

NP0, NP1, NP2 = 176, 56, 24
FACES = 4
AGG = 8
HLEV = 2
HALO = 512
EC_DEV = 256
E_DEV = 2048
LANES = 128
PAIR = 256
PAIRS = E_DEV // PAIR
SIDE = HALO // PAIR
SPAN = 2 * SIDE + 1
EXT = PAIRS + 2 * SIDE
ROWS_PER = E_DEV // LANES
DAMPING = 0.8
NPM = 64
NPL = 32
KF = 896
KM = 5 * NPM
KL = 5 * NPL
MX_ROWS = 112
MX_FACES = 2
MESH = pl.DeviceIdType.MESH
F32, BF16 = jnp.float32, jnp.bfloat16
NN = (((1,), (0,)), ((), ()))
NT = (((1,), (1,)), ((), ()))


def exact(a, b, dims=NN):
    return lax.dot_general(a, b, dims, precision=lax.Precision.HIGHEST, preferred_element_type=F32)


def parts(x):
    high = x.astype(BF16)
    low = (x - high.astype(F32)).astype(BF16)
    return high, low


def store_parts(ref, x, rows):
    high, low = parts(x)
    ref[pl.ds(0, x.shape[0]), :] = high
    ref[pl.ds(rows, x.shape[0]), :] = low


def product(split_ref, rows, high, low):
    both = jnp.dot(split_ref[...], high, preferred_element_type=F32)
    rest = jnp.dot(split_ref[pl.ds(0, rows), :], low, preferred_element_type=F32)
    return both[:rows] + both[rows:] + rest


def kernel(
    n_dom,
    n_fold,
    iter_ref,
    rhs_ref,
    jac_ref,
    scale_ref,
    offset_ref,
    agg_ref,
    live_ref,
    stiff_ref,
    flux_ref,
    smoother_ref,
    rmid_ref,
    rlow_ref,
    upd_ref,
    res_ref,
    e1,
    e2,
    e3,
    e4,
    e5,
    split1,
    split2,
    pick,
    second,
    split3,
    split5,
    mid_rhs,
    low_rhs,
    low_res,
    feed_high,
    feed_low,
    feed_mid,
    feed_coarse,
    fine_f32,
    fine_split,
    smooth_split,
    rmid_split,
    rboth_split,
    mid_split,
    lift_f32,
    lift_split,
    low_split,
    rmid_t_split,
    low_t_f32,
    swap_out,
    swap_in,
    send_sem,
    recv_sem,
    swap_send,
    swap_recv,
):
    me = lax.axis_index("dom")
    fold = lax.axis_index("fold")
    right = lax.rem(me + 1, n_dom)
    left = lax.rem(me + n_dom - 1, n_dom)
    partners = []
    for height in range(HLEV):
        step = 2**height
        bit = (fold // step) % 2
        partners.append(fold + step - 2 * step * bit)

    barrier = pltpu.get_barrier_semaphore()
    for other in (left, right):
        pl.semaphore_signal(barrier, inc=1, device_id={"dom": other}, device_id_type=MESH)
    for other in partners:
        pl.semaphore_signal(barrier, inc=1, device_id={"fold": other}, device_id_type=MESH)

    lane = lax.broadcasted_iota(jnp.int32, (1, PAIR), 1)
    live = live_ref[0, 0]

    def row_of(ref, base, u):
        return jnp.concatenate(
            [ref[pl.ds(base + 2 * u, 1), :], ref[pl.ds(base + 2 * u + 1, 1), :]], axis=1
        )

    def active_of(u):
        return jnp.where(u * PAIR + lane < live, 1.0, 0.0).astype(F32)

    def jac_of(u):
        return row_of(jac_ref, 0, u)

    def weight_of(f, u):
        offset = row_of(offset_ref, f * ROWS_PER, u)
        target = me * E_DEV + u * PAIR + lane + offset
        inside = (offset != 0) & (target >= 0) & (target < n_dom * E_DEV)
        return jnp.where(inside, row_of(scale_ref, f * ROWS_PER, u), 0.0)

    def wide(ref, u):
        return jnp.concatenate(
            [ref[pl.ds(2 * u + h, NP0, stride=ROWS_PER), :] for h in range(2)], axis=1
        )

    def put_wide(ref, u, value):
        for h in range(2):
            ref[pl.ds(2 * u + h, NP0, stride=ROWS_PER), :] = value[:, h * LANES : (h + 1) * LANES]

    def exchange(k, buffer):
        to_right = pltpu.make_async_remote_copy(
            src_ref=buffer.at[pl.ds(PAIRS, SIDE)],
            dst_ref=buffer.at[pl.ds(0, SIDE)],
            send_sem=send_sem.at[k, 0],
            recv_sem=recv_sem.at[k, 0],
            device_id={"dom": right},
            device_id_type=MESH,
        )
        to_left = pltpu.make_async_remote_copy(
            src_ref=buffer.at[pl.ds(SIDE, SIDE)],
            dst_ref=buffer.at[pl.ds(SIDE + PAIRS, SIDE)],
            send_sem=send_sem.at[k, 1],
            recv_sem=recv_sem.at[k, 1],
            device_id={"dom": left},
            device_id_type=MESH,
        )
        to_right.start()
        to_left.start()
        return to_right, to_left

    def finish(copies):
        for copy in copies:
            copy.wait()

    def over(first, last, body):
        lax.fori_loop(first, last, lambda i, c: (body(i), c)[1], 0)

    def over_edges(body):
        lax.fori_loop(
            0, 2 * SIDE, lambda i, c: (body(i + (i // SIDE) * (PAIRS - 2 * SIDE)), c)[1], 0
        )

    def mask_block(u):
        e1[u + SIDE] = active_of(u) * wide(iter_ref, u)

    over(0, PAIRS, mask_block)
    pl.semaphore_wait(barrier, 2 + HLEV)
    first_halo = exchange(0, e1)

    def split_block(source, target, b):
        store_parts(target.at[b], source[b, pl.ds(0, MX_ROWS), :], MX_ROWS)

    def split_mid(target, b, value):
        padded = jnp.concatenate([value, jnp.zeros((NPM - NP1, PAIR), F32)], axis=0)
        store_parts(target.at[b], padded, NPM)

    halo_blocks = (*range(SIDE), *range(SIDE + PAIRS, EXT))

    def split_halo(source, target):
        for b in halo_blocks:
            split_block(source, target, b)

    over(SIDE, SIDE + PAIRS, lambda b: split_block(e1, split1, b))

    fine_f32[...] = jnp.zeros_like(fine_f32)
    for f in range(FACES):
        fine_f32[:, f * NP0 : (f + 1) * NP0] = flux_ref[f]
    fine_f32[:, FACES * NP0 : (FACES + 1) * NP0] = stiff_ref[...]
    store_parts(fine_split, fine_f32[...], NP0)
    store_parts(smooth_split, smoother_ref[...], NP0)
    feed_high[...] = jnp.zeros_like(feed_high)
    feed_low[...] = jnp.zeros_like(feed_low)

    def build_pick(u, f):
        reach = lane + row_of(offset_ref, f * ROWS_PER, u) + HALO
        rows = lax.broadcasted_iota(jnp.int32, (PAIR, PAIR), 0)
        for j in range(SPAN):
            pick[u, f, pl.ds(j * PAIR, PAIR), :] = jnp.where(
                rows + j * PAIR == reach, 1.0, 0.0
            ).astype(BF16)

    reach_lane = lax.broadcasted_iota(jnp.int32, (8, LANES), 1)

    def lane_gather(u, buffer, f, first, rows, padding=0):
        halves = []
        for h in range(2):
            offset = offset_ref[pl.ds(f * ROWS_PER + 2 * u + h, 1), :]
            reach = jnp.broadcast_to(offset, (8, LANES)) + reach_lane + HALO
            inner = reach & (LANES - 1)
            outer = reach >> 7
            groups = []
            for g in range(rows // 8):
                value = None
                for j in range(2 * HALO // LANES + 1):
                    b = h + j
                    source = buffer[
                        u + b // 2, pl.ds(first + 8 * g, 8), pl.ds((b % 2) * LANES, LANES)
                    ]
                    found = jnp.take_along_axis(source, inner, axis=1)
                    value = found if j == 0 else jnp.where(outer == j, found, value)
                groups.append(value)
            if padding:
                groups.append(jnp.zeros((padding, LANES), F32))
            halves.append(jnp.concatenate(groups, axis=0))
        return jnp.concatenate(halves, axis=1)

    def fine_apply(u, source, split, build):
        around = jnp.concatenate([split[u + j] for j in range(SPAN)], axis=1)
        for f in range(FACES):
            if build:
                build_pick(u, f)
            weight = weight_of(f, u)
            both = jnp.dot(around, pick[u, f], preferred_element_type=F32)
            high, low = parts((both[:MX_ROWS] + both[MX_ROWS:]) * weight)
            feed_high[pl.ds(f * NP0, MX_ROWS), :] = high
            feed_low[pl.ds(f * NP0, MX_ROWS), :] = low
            rest = lane_gather(u, source, f, MX_ROWS, NP0 - MX_ROWS)
            high, low = parts(rest * weight)
            feed_high[pl.ds(f * NP0 + MX_ROWS, NP0 - MX_ROWS), :] = high
            feed_low[pl.ds(f * NP0 + MX_ROWS, NP0 - MX_ROWS), :] = low
        high, low = parts(jac_of(u) * source[u + SIDE])
        feed_high[pl.ds(FACES * NP0, NP0), :] = high
        feed_low[pl.ds(FACES * NP0, NP0), :] = low
        return product(fine_split, NP0, feed_high[...], feed_low[...])

    def smooth_block(u):
        active = active_of(u)
        first_res = active * (wide(rhs_ref, u) - fine_apply(u, e1, split1, True))
        high, low = parts(first_res)
        update = product(smooth_split, NP0, high, low)
        block = e1[u + SIDE] + update * (active / jac_of(u))
        e2[u + SIDE] = block
        store_parts(split2.at[u + SIDE], block[:MX_ROWS], MX_ROWS)

    over(SIDE, PAIRS - SIDE, smooth_block)
    finish(first_halo)
    split_halo(e1, split1)
    over_edges(smooth_block)
    second_halo = exchange(1, e2)

    rmid = rmid_ref[...]
    rlow = rlow_ref[...]
    rboth = exact(rlow, rmid)
    lift_f32[...] = jnp.zeros_like(lift_f32)
    low_t_f32[...] = jnp.zeros_like(low_t_f32)
    rmid_t_split[...] = jnp.zeros_like(rmid_t_split)

    def identity(n):
        rows = lax.broadcasted_iota(jnp.int32, (n, n), 0)
        cols = lax.broadcasted_iota(jnp.int32, (n, n), 1)
        return jnp.where(rows == cols, 1.0, 0.0).astype(F32)

    def below(value, rows):
        return jnp.concatenate([value, jnp.zeros((rows, value.shape[1]), F32)], axis=0)

    def turned(value):
        unit = identity(value.shape[1]).astype(BF16)
        return [
            lax.dot_general(unit, part, NT, preferred_element_type=F32).astype(BF16)
            for part in parts(value)
        ]

    store_parts(rmid_split, below(rmid, NPM - NP1), NPM)
    store_parts(rboth_split, below(rboth, NPL - NP2), NPL)
    stacked = jnp.concatenate([below(rmid, NPM - NP1), below(rboth, NPL - NP2)], axis=0)
    stacked_high, stacked_low = turned(stacked)
    for f in range(FACES + 1):
        high, low = parts(flux_ref[f] if f < FACES else stiff_ref[...])
        lifted = (
            jnp.dot(high, stacked_high, preferred_element_type=F32)
            + jnp.dot(low, stacked_high, preferred_element_type=F32)
            + jnp.dot(high, stacked_low, preferred_element_type=F32)
        )
        lift_f32[:, f * NPM : (f + 1) * NPM] = lifted[:, :NPM]
        low_t_f32[:, f * NPL : (f + 1) * NPL] = lifted[:, NPM : NPM + NPL]
    lift = lift_f32[...]
    store_parts(lift_split, lift, NP0)
    mid_matrix = product(rmid_split, NPM, *parts(lift))
    low_matrix = product(rboth_split, NPL, *parts(low_t_f32[...]))
    store_parts(mid_split, mid_matrix, NPM)
    store_parts(low_split, low_matrix, NPL)
    mid_own = mid_matrix[:NP1, FACES * NPM : FACES * NPM + NP1]
    stiff_low = low_matrix[:NP2, FACES * NPL : FACES * NPL + NP2]
    diag_mid = jnp.sum(mid_own * identity(NP1), axis=1, keepdims=True)
    diag_low = jnp.sum(stiff_low * identity(NP2), axis=1, keepdims=True)
    rmid_t_split[pl.ds(0, NP0), :] = stacked_high[:, :NPM]
    rmid_t_split[pl.ds(NP0, NP0), :] = stacked_low[:, :NPM]
    rlow_t_high, rlow_t_low = turned(below(rlow, NPL - NP2))
    rlow_t = jnp.concatenate([rlow_t_high, rlow_t_low], axis=0)

    def second_block(u):
        active = active_of(u)
        block = active * (wide(rhs_ref, u) - fine_apply(u, e2, split2, False))
        second[u] = block
        high, low = parts(block)
        rhs = product(rmid_split, NPM, high, low)[:NP1]
        mid_rhs[u] = rhs
        corr = rhs * (DAMPING * active / jac_of(u)) / diag_mid
        e3[u + SIDE] = corr
        split_mid(split3, u + SIDE, corr)

    over(SIDE, PAIRS - SIDE, second_block)
    finish(second_halo)
    split_halo(e2, split2)
    over_edges(second_block)
    mid_halo = exchange(2, e3)

    def mid_feed(u, buffer, split):
        around = jnp.concatenate([split[u + j] for j in range(SPAN)], axis=1)
        for f in range(FACES):
            if f < MX_FACES:
                both = jnp.dot(around, pick[u, f], preferred_element_type=F32)
                value = both[:NPM] + both[NPM:]
            else:
                value = lane_gather(u, buffer, f, 0, NP1, NPM - NP1)
            high, low = parts(value * weight_of(f, u))
            feed_mid[0, pl.ds(f * NPM, NPM), :] = high
            feed_mid[1, pl.ds(f * NPM, NPM), :] = low
        high, low = parts(below(jac_of(u) * buffer[u + SIDE], NPM - NP1))
        feed_mid[0, pl.ds(FACES * NPM, NPM), :] = high
        feed_mid[1, pl.ds(FACES * NPM, NPM), :] = low
        return feed_mid[0], feed_mid[1]

    def low_feed(u, buffer):
        for f in range(FACES):
            value = lane_gather(u, buffer, f, 0, NP2, NPL - NP2)
            high, low = parts(value * weight_of(f, u))
            feed_coarse[0, pl.ds(f * NPL, NPL), :] = high
            feed_coarse[1, pl.ds(f * NPL, NPL), :] = low
        high, low = parts(below(jac_of(u) * buffer[u + SIDE], NPL - NP2))
        feed_coarse[0, pl.ds(FACES * NPL, NPL), :] = high
        feed_coarse[1, pl.ds(FACES * NPL, NPL), :] = low
        return feed_coarse[0], feed_coarse[1]

    def mid_block(u):
        active = active_of(u)
        high, low = mid_feed(u, e3, split3)
        mid_res = mid_rhs[u] - active * product(mid_split, NPM, high, low)[:NP1]
        rhs = exact(rlow, mid_res)
        low_rhs[u] = rhs
        e4[u + SIDE] = rhs * (DAMPING * active / jac_of(u)) / diag_low

    over(SIDE, PAIRS - SIDE, mid_block)
    finish(mid_halo)
    for b in halo_blocks:
        split_mid(split3, b, e3[b])
    over_edges(mid_block)
    low_halo = exchange(3, e4)

    def low_block(u):
        active = active_of(u)
        high, low = low_feed(u, e4)
        low_res[u] = low_rhs[u] - active * product(low_split, NPL, high, low)[:NP2]

    over(SIDE, PAIRS - SIDE, low_block)
    finish(low_halo)
    over_edges(low_block)

    def members(u):
        rows = lax.broadcasted_iota(jnp.int32, (EC_DEV, PAIR), 0)
        return jnp.where(rows == row_of(agg_ref, 0, u), 1.0, 0.0).astype(BF16)

    def coarse_block(u, total):
        high, low = parts(
            jnp.concatenate([low_res[u], jnp.zeros((NPL - NP2, PAIR), F32)], axis=0)
        )
        both = lax.dot_general(
            jnp.concatenate([high, low], axis=0), members(u), NT, preferred_element_type=F32
        )
        return total + both[:NP2] + both[NPL : NPL + NP2]

    coarse = lax.fori_loop(0, PAIRS, coarse_block, jnp.zeros((NP2, EC_DEV), F32))
    sections = []
    for height in range(HLEV):
        scaled = coarse / diag_low
        sections.append(scaled * (DAMPING / (AGG * 2**height)))
        residue = coarse - DAMPING * exact(stiff_low, scaled)
        swap_out[height] = residue
        copy = pltpu.make_async_remote_copy(
            src_ref=swap_out.at[height],
            dst_ref=swap_in.at[height],
            send_sem=swap_send.at[height],
            recv_sem=swap_recv.at[height],
            device_id={"fold": partners[height]},
            device_id_type=MESH,
        )
        copy.start()
        copy.wait()
        coarse = residue + swap_in[height]
    corr = coarse / diag_low * (DAMPING / (AGG * 2**HLEV))
    for height in reversed(range(HLEV)):
        corr = sections[height] + corr
    corr_high, corr_low = parts(jnp.concatenate([corr, jnp.zeros((NPL - NP2, EC_DEV), F32)], axis=0))
    corr_split = jnp.concatenate([corr_high, corr_low], axis=0)

    def ascend_block(u):
        active = active_of(u)
        both = jnp.dot(corr_split, members(u), preferred_element_type=F32)
        low_total = e4[u + SIDE] + active * (both[:NP2] + both[NPL : NPL + NP2])
        high, low = parts(below(low_total, NPL - NP2))
        up = jnp.dot(rlow_t, high, preferred_element_type=F32)
        up = up[:NP1] + up[NP1:] + jnp.dot(rlow_t[:NP1], low, preferred_element_type=F32)
        total = e3[u + SIDE] + up
        e5[u + SIDE] = total
        split_mid(split5, u + SIDE, total)

    over_edges(ascend_block)
    last_halo = exchange(4, e5)
    over(SIDE, PAIRS - SIDE, ascend_block)

    def update_block(u):
        high, low = split5[u + SIDE, pl.ds(0, NPM), :], split5[u + SIDE, pl.ds(NPM, NPM), :]
        put_wide(upd_ref, u, e2[u + SIDE] + product(rmid_t_split, NP0, high, low))

    over(0, PAIRS, update_block)

    def residual_block(u):
        high, low = mid_feed(u, e5, split5)
        put_wide(res_ref, u, second[u] - active_of(u) * product(lift_split, NP0, high, low))

    over(SIDE, PAIRS - SIDE, residual_block)
    finish(last_halo)
    for b in halo_blocks:
        split_mid(split5, b, e5[b])
    over_edges(residual_block)


def on_device(
    n_dom,
    n_fold,
    iterate,
    right_side,
    jacobian,
    face_scale,
    face_offset,
    agglomerate,
    live_count,
    stiff_fine,
    flux_fine,
    smoother,
    restrict_mid,
    restrict_low,
):
    def flat(array):
        return array.reshape(-1, LANES)

    vmem = pl.BlockSpec(memory_space=pltpu.VMEM)
    smem = pl.BlockSpec(memory_space=pltpu.SMEM)
    out = jax.ShapeDtypeStruct((NP0 * ROWS_PER, LANES), F32)
    updated, residual = pl.pallas_call(
        partial(kernel, n_dom, n_fold),
        out_shape=(out, out),
        in_specs=[vmem] * 6 + [smem] + [vmem] * 5,
        out_specs=(vmem, vmem),
        scratch_shapes=[
            pltpu.VMEM((EXT, NP0, PAIR), F32),
            pltpu.VMEM((EXT, NP0, PAIR), F32),
            pltpu.VMEM((EXT, NP1, PAIR), F32),
            pltpu.VMEM((EXT, NP2, PAIR), F32),
            pltpu.VMEM((EXT, NP1, PAIR), F32),
            pltpu.VMEM((EXT, 2 * MX_ROWS, PAIR), BF16),
            pltpu.VMEM((EXT, 2 * MX_ROWS, PAIR), BF16),
            pltpu.VMEM((PAIRS, FACES, SPAN * PAIR, PAIR), BF16),
            pltpu.VMEM((PAIRS, NP0, PAIR), F32),
            pltpu.VMEM((EXT, 2 * NPM, PAIR), BF16),
            pltpu.VMEM((EXT, 2 * NPM, PAIR), BF16),
            pltpu.VMEM((PAIRS, NP1, PAIR), F32),
            pltpu.VMEM((PAIRS, NP2, PAIR), F32),
            pltpu.VMEM((PAIRS, NP2, PAIR), F32),
            pltpu.VMEM((KF, PAIR), BF16),
            pltpu.VMEM((KF, PAIR), BF16),
            pltpu.VMEM((2, KM, PAIR), BF16),
            pltpu.VMEM((2, KL, PAIR), BF16),
            pltpu.VMEM((NP0, KF), F32),
            pltpu.VMEM((2 * NP0, KF), BF16),
            pltpu.VMEM((2 * NP0, NP0), BF16),
            pltpu.VMEM((2 * NPM, NP0), BF16),
            pltpu.VMEM((2 * NPL, NP0), BF16),
            pltpu.VMEM((2 * NPM, KM), BF16),
            pltpu.VMEM((NP0, KM), F32),
            pltpu.VMEM((2 * NP0, KM), BF16),
            pltpu.VMEM((2 * NPL, KL), BF16),
            pltpu.VMEM((2 * NP0, NPM), BF16),
            pltpu.VMEM((NP0, KL), F32),
            pltpu.VMEM((HLEV, NP2, EC_DEV), F32),
            pltpu.VMEM((HLEV, NP2, EC_DEV), F32),
            pltpu.SemaphoreType.DMA((5, 2)),
            pltpu.SemaphoreType.DMA((5, 2)),
            pltpu.SemaphoreType.DMA((HLEV,)),
            pltpu.SemaphoreType.DMA((HLEV,)),
        ],
        compiler_params=pltpu.CompilerParams(
            collective_id=0, has_side_effects=True, vmem_limit_bytes=44 * 1024 * 1024
        ),
    )(
        flat(iterate),
        flat(right_side),
        flat(jacobian),
        flat(face_scale),
        flat(face_offset),
        flat(agglomerate),
        live_count,
        stiff_fine,
        flux_fine,
        smoother,
        restrict_mid,
        restrict_low,
    )
    return updated.reshape(iterate.shape), residual.reshape(iterate.shape)


def solution(mesh):
    return jax.shard_map(
        partial(on_device, mesh.shape["dom"], mesh.shape["fold"]),
        mesh=mesh,
        in_specs=(
            P(None, "fold", "dom"),
            P(None, "fold", "dom"),
            P("fold", "dom"),
            P(None, "fold", "dom"),
            P(None, "fold", "dom"),
            P("fold", "dom"),
            P("fold", "dom"),
            P(),
            P(),
            P(),
            P(),
            P(),
        ),
        out_specs=(P(None, "fold", "dom"), P(None, "fold", "dom")),
        check_vma=False,
    )
```

```python
from functools import partial

import jax
import jax.numpy as jnp
from jax import lax
from jax.experimental import pallas as pl
from jax.experimental.pallas import tpu as pltpu
from jax.sharding import PartitionSpec as P

NP0, NP1, NP2 = 176, 56, 24
FACES = 4
AGG = 8
HLEV = 2
HALO = 512
EC_DEV = 256
E_DEV = 2048
LANES = 128
PAIR = 256
PAIRS = E_DEV // PAIR
SIDE = HALO // PAIR
SPAN = 2 * SIDE + 1
EXT = PAIRS + 2 * SIDE
ROWS_PER = E_DEV // LANES
DAMPING = 0.8
NPM = 64
NPL = 32
KF = 896
KM = 5 * NPM
KL = 5 * NPL
MX_ROWS = 112
MX_FACES = 2
MESH = pl.DeviceIdType.MESH
F32, BF16 = jnp.float32, jnp.bfloat16
NN = (((1,), (0,)), ((), ()))
NT = (((1,), (1,)), ((), ()))


def exact(a, b, dims=NN):
    return lax.dot_general(a, b, dims, precision=lax.Precision.HIGHEST, preferred_element_type=F32)


def parts(x):
    high = x.astype(BF16)
    low = (x - high.astype(F32)).astype(BF16)
    return high, low


def store_parts(ref, x, rows):
    high, low = parts(x)
    ref[pl.ds(0, x.shape[0]), :] = high
    ref[pl.ds(rows, x.shape[0]), :] = low


def product(split_ref, rows, high, low):
    both = jnp.dot(split_ref[...], high, preferred_element_type=F32)
    rest = jnp.dot(split_ref[pl.ds(0, rows), :], low, preferred_element_type=F32)
    return both[:rows] + both[rows:] + rest


def kernel(
    n_dom,
    n_fold,
    iter_hbm,
    rhs_hbm,
    jac_hbm,
    scale_hbm,
    offset_hbm,
    agg_hbm,
    live_ref,
    stiff_hbm,
    flux_hbm,
    smoother_hbm,
    rmid_hbm,
    rlow_hbm,
    upd_ref,
    res_ref,
    iter_ref,
    rhs_ref,
    jac_ref,
    scale_ref,
    offset_ref,
    agg_ref,
    stiff_ref,
    flux_ref,
    smoother_ref,
    rmid_ref,
    rlow_ref,
    e1,
    e2,
    e3,
    e4,
    e5,
    split1,
    split2,
    pick,
    second,
    split3,
    split5,
    mid_rhs,
    low_rhs,
    coarse_sum,
    feed_high,
    feed_low,
    feed_mid,
    feed_coarse,
    fine_f32,
    fine_split,
    smooth_split,
    rmid_split,
    rboth_split,
    mid_split,
    lift_f32,
    lift_split,
    low_split,
    rmid_t_split,
    low_t_f32,
    swap_out,
    swap_in,
    send_sem,
    recv_sem,
    swap_send,
    swap_recv,
    load_sem,
):
    me = lax.axis_index("dom")
    fold = lax.axis_index("fold")
    right = lax.rem(me + 1, n_dom)
    left = lax.rem(me + n_dom - 1, n_dom)
    low_bit, high_bit = fold % 2, (fold // 2) % 2
    flip = fold + 1 - 2 * low_bit
    across = 2 - 4 * high_bit
    partners = (flip, fold + across, flip + across)

    loads = [
        pltpu.make_async_copy(source, target, load_sem.at[i])
        for i, (source, target) in enumerate(
            (
                (iter_hbm, iter_ref),
                (offset_hbm, offset_ref),
                (flux_hbm, flux_ref),
                (stiff_hbm, stiff_ref),
                (smoother_hbm, smoother_ref),
                (scale_hbm, scale_ref),
                (jac_hbm, jac_ref),
                (rhs_hbm, rhs_ref),
                (rmid_hbm, rmid_ref),
                (rlow_hbm, rlow_ref),
                (agg_hbm, agg_ref),
            )
        )
    ]
    for load in loads:
        load.start()

    barrier = pltpu.get_barrier_semaphore()
    for other in (left, right):
        pl.semaphore_signal(barrier, inc=1, device_id={"dom": other}, device_id_type=MESH)
    for other in partners:
        pl.semaphore_signal(barrier, inc=1, device_id={"fold": other}, device_id_type=MESH)

    lane = lax.broadcasted_iota(jnp.int32, (1, PAIR), 1)
    live = live_ref[0, 0]

    def row_of(ref, base, u):
        return jnp.concatenate(
            [ref[pl.ds(base + 2 * u, 1), :], ref[pl.ds(base + 2 * u + 1, 1), :]], axis=1
        )

    def active_of(u):
        return jnp.where(u * PAIR + lane < live, 1.0, 0.0).astype(F32)

    def jac_of(u):
        return row_of(jac_ref, 0, u)

    def weight_of(f, u):
        offset = row_of(offset_ref, f * ROWS_PER, u)
        target = me * E_DEV + u * PAIR + lane + offset
        inside = (offset != 0) & (target >= 0) & (target < n_dom * E_DEV)
        return jnp.where(inside, row_of(scale_ref, f * ROWS_PER, u), 0.0)

    def wide(ref, u):
        return jnp.concatenate(
            [ref[pl.ds(2 * u + h, NP0, stride=ROWS_PER), :] for h in range(2)], axis=1
        )

    def put_wide(ref, u, value):
        for h in range(2):
            ref[pl.ds(2 * u + h, NP0, stride=ROWS_PER), :] = value[:, h * LANES : (h + 1) * LANES]

    pending = []

    def send(k, buffer, side):
        copy = pltpu.make_async_remote_copy(
            src_ref=buffer.at[pl.ds(PAIRS if side == 0 else SIDE, SIDE)],
            dst_ref=buffer.at[pl.ds(0 if side == 0 else SIDE + PAIRS, SIDE)],
            send_sem=send_sem.at[k, side],
            recv_sem=recv_sem.at[k, side],
            device_id={"dom": right if side == 0 else left},
            device_id_type=MESH,
        )
        copy.start()
        pending.append(copy)
        return copy

    def over(first, last, body):
        lax.fori_loop(first, last, lambda i, c: (body(i), c)[1], 0)

    def over_left(body):
        over(0, SIDE, body)

    def over_right(body):
        over(PAIRS - SIDE, PAIRS, body)

    def mask_block(u):
        e1[u + SIDE] = active_of(u) * wide(iter_ref, u)

    loads[0].wait()
    over_left(mask_block)
    over_right(mask_block)
    pl.semaphore_wait(barrier, 2 + len(partners))
    from_left = send(0, e1, 0)
    from_right = send(0, e1, 1)
    over(SIDE, PAIRS - SIDE, mask_block)
    for load in loads[1:]:
        load.wait()

    def split_block(source, target, b):
        store_parts(target.at[b], source[b, pl.ds(0, MX_ROWS), :], MX_ROWS)

    def split_mid(target, b, value):
        padded = jnp.concatenate([value, jnp.zeros((NPM - NP1, PAIR), F32)], axis=0)
        store_parts(target.at[b], padded, NPM)

    left_halo = tuple(range(SIDE))
    right_halo = tuple(range(SIDE + PAIRS, EXT))

    over(SIDE, SIDE + PAIRS, lambda b: split_block(e1, split1, b))

    fine_f32[...] = jnp.zeros_like(fine_f32)
    for f in range(FACES):
        fine_f32[:, f * NP0 : (f + 1) * NP0] = flux_ref[f]
    fine_f32[:, FACES * NP0 : (FACES + 1) * NP0] = stiff_ref[...]
    store_parts(fine_split, fine_f32[...], NP0)
    store_parts(smooth_split, smoother_ref[...], NP0)
    feed_high[...] = jnp.zeros_like(feed_high)
    feed_low[...] = jnp.zeros_like(feed_low)

    def build_pick(u, f):
        reach = lane + row_of(offset_ref, f * ROWS_PER, u) + HALO
        rows = lax.broadcasted_iota(jnp.int32, (PAIR, PAIR), 0)
        for j in range(SPAN):
            pick[u, f, pl.ds(j * PAIR, PAIR), :] = jnp.where(
                rows + j * PAIR == reach, 1.0, 0.0
            ).astype(BF16)

    reach_lane = lax.broadcasted_iota(jnp.int32, (8, LANES), 1)

    def lane_gather(u, buffer, f, first, rows, padding=0):
        halves = []
        for h in range(2):
            offset = offset_ref[pl.ds(f * ROWS_PER + 2 * u + h, 1), :]
            reach = jnp.broadcast_to(offset, (8, LANES)) + reach_lane + HALO
            inner = reach & (LANES - 1)
            outer = reach >> 7
            groups = []
            for g in range(rows // 8):
                value = None
                for j in range(2 * HALO // LANES + 1):
                    b = h + j
                    source = buffer[
                        u + b // 2, pl.ds(first + 8 * g, 8), pl.ds((b % 2) * LANES, LANES)
                    ]
                    found = jnp.take_along_axis(source, inner, axis=1)
                    value = found if j == 0 else jnp.where(outer == j, found, value)
                groups.append(value)
            if padding:
                groups.append(jnp.zeros((padding, LANES), F32))
            halves.append(jnp.concatenate(groups, axis=0))
        return jnp.concatenate(halves, axis=1)

    def fine_apply(u, source, split, build):
        around = jnp.concatenate([split[u + j] for j in range(SPAN)], axis=1)
        for f in range(FACES):
            if build:
                build_pick(u, f)
            weight = weight_of(f, u)
            both = jnp.dot(around, pick[u, f], preferred_element_type=F32)
            high, low = parts((both[:MX_ROWS] + both[MX_ROWS:]) * weight)
            feed_high[pl.ds(f * NP0, MX_ROWS), :] = high
            feed_low[pl.ds(f * NP0, MX_ROWS), :] = low
            rest = lane_gather(u, source, f, MX_ROWS, NP0 - MX_ROWS)
            high, low = parts(rest * weight)
            feed_high[pl.ds(f * NP0 + MX_ROWS, NP0 - MX_ROWS), :] = high
            feed_low[pl.ds(f * NP0 + MX_ROWS, NP0 - MX_ROWS), :] = low
        high, low = parts(jac_of(u) * source[u + SIDE])
        feed_high[pl.ds(FACES * NP0, NP0), :] = high
        feed_low[pl.ds(FACES * NP0, NP0), :] = low
        return product(fine_split, NP0, feed_high[...], feed_low[...])

    def smooth_block(u):
        active = active_of(u)
        first_res = active * (wide(rhs_ref, u) - fine_apply(u, e1, split1, True))
        high, low = parts(first_res)
        update = product(smooth_split, NP0, high, low)
        block = e1[u + SIDE] + update * (active / jac_of(u))
        e2[u + SIDE] = block
        store_parts(split2.at[u + SIDE], block[:MX_ROWS], MX_ROWS)

    over(SIDE, PAIRS - SIDE, smooth_block)

    rmid = rmid_ref[...]
    rlow = rlow_ref[...]
    rboth = exact(rlow, rmid)
    lift_f32[...] = jnp.zeros_like(lift_f32)
    low_t_f32[...] = jnp.zeros_like(low_t_f32)
    rmid_t_split[...] = jnp.zeros_like(rmid_t_split)

    def identity(n):
        rows = lax.broadcasted_iota(jnp.int32, (n, n), 0)
        cols = lax.broadcasted_iota(jnp.int32, (n, n), 1)
        return jnp.where(rows == cols, 1.0, 0.0).astype(F32)

    def below(value, rows):
        return jnp.concatenate([value, jnp.zeros((rows, value.shape[1]), F32)], axis=0)

    def turned(value):
        unit = identity(value.shape[1]).astype(BF16)
        return [
            lax.dot_general(unit, part, NT, preferred_element_type=F32).astype(BF16)
            for part in parts(value)
        ]

    store_parts(rmid_split, below(rmid, NPM - NP1), NPM)
    store_parts(rboth_split, below(rboth, NPL - NP2), NPL)
    stacked = jnp.concatenate([below(rmid, NPM - NP1), below(rboth, NPL - NP2)], axis=0)
    stacked_high, stacked_low = turned(stacked)
    for f in range(FACES + 1):
        high, low = parts(flux_ref[f] if f < FACES else stiff_ref[...])
        lifted = (
            jnp.dot(high, stacked_high, preferred_element_type=F32)
            + jnp.dot(low, stacked_high, preferred_element_type=F32)
            + jnp.dot(high, stacked_low, preferred_element_type=F32)
        )
        lift_f32[:, f * NPM : (f + 1) * NPM] = lifted[:, :NPM]
        low_t_f32[:, f * NPL : (f + 1) * NPL] = lifted[:, NPM : NPM + NPL]
    lift = lift_f32[...]
    store_parts(lift_split, lift, NP0)
    mid_matrix = product(rmid_split, NPM, *parts(lift))
    low_matrix = product(rboth_split, NPL, *parts(low_t_f32[...]))
    store_parts(mid_split, mid_matrix, NPM)
    store_parts(low_split, low_matrix, NPL)
    mid_own = mid_matrix[:NP1, FACES * NPM : FACES * NPM + NP1]
    stiff_low = low_matrix[:NP2, FACES * NPL : FACES * NPL + NP2]
    diag_mid = jnp.sum(mid_own * identity(NP1), axis=1, keepdims=True)
    diag_low = jnp.sum(stiff_low * identity(NP2), axis=1, keepdims=True)
    rmid_t_split[pl.ds(0, NP0), :] = stacked_high[:, :NPM]
    rmid_t_split[pl.ds(NP0, NP0), :] = stacked_low[:, :NPM]
    rlow_t_high, rlow_t_low = turned(below(rlow, NPL - NP2))
    rlow_t = jnp.concatenate([rlow_t_high, rlow_t_low], axis=0)

    from_left.wait_recv()
    for b in left_halo:
        split_block(e1, split1, b)
    over_left(smooth_block)
    to_left = send(1, e2, 1)
    from_right.wait_recv()
    for b in right_halo:
        split_block(e1, split1, b)
    over_right(smooth_block)
    to_right = send(1, e2, 0)

    def second_block(u):
        active = active_of(u)
        block = active * (wide(rhs_ref, u) - fine_apply(u, e2, split2, False))
        second[u] = block
        high, low = parts(block)
        rhs = product(rmid_split, NPM, high, low)[:NP1]
        mid_rhs[u] = rhs
        corr = rhs * (DAMPING * active / jac_of(u)) / diag_mid
        e3[u + SIDE] = corr
        split_mid(split3, u + SIDE, corr)

    over(SIDE, PAIRS - SIDE, second_block)
    to_left.wait_recv()
    for b in right_halo:
        split_block(e2, split2, b)
    over_right(second_block)
    mid_right = send(2, e3, 0)
    to_right.wait_recv()
    for b in left_halo:
        split_block(e2, split2, b)
    over_left(second_block)
    mid_left = send(2, e3, 1)

    def mid_feed(u, buffer, split):
        around = jnp.concatenate([split[u + j] for j in range(SPAN)], axis=1)
        for f in range(FACES):
            if f < MX_FACES:
                both = jnp.dot(around, pick[u, f], preferred_element_type=F32)
                value = both[:NPM] + both[NPM:]
            else:
                value = lane_gather(u, buffer, f, 0, NP1, NPM - NP1)
            high, low = parts(value * weight_of(f, u))
            feed_mid[0, pl.ds(f * NPM, NPM), :] = high
            feed_mid[1, pl.ds(f * NPM, NPM), :] = low
        high, low = parts(below(jac_of(u) * buffer[u + SIDE], NPM - NP1))
        feed_mid[0, pl.ds(FACES * NPM, NPM), :] = high
        feed_mid[1, pl.ds(FACES * NPM, NPM), :] = low
        return feed_mid[0], feed_mid[1]

    def low_feed(u, buffer):
        for f in range(FACES):
            value = lane_gather(u, buffer, f, 0, NP2, NPL - NP2)
            high, low = parts(value * weight_of(f, u))
            feed_coarse[0, pl.ds(f * NPL, NPL), :] = high
            feed_coarse[1, pl.ds(f * NPL, NPL), :] = low
        high, low = parts(below(jac_of(u) * buffer[u + SIDE], NPL - NP2))
        feed_coarse[0, pl.ds(FACES * NPL, NPL), :] = high
        feed_coarse[1, pl.ds(FACES * NPL, NPL), :] = low
        return feed_coarse[0], feed_coarse[1]

    def mid_block(u):
        active = active_of(u)
        high, low = mid_feed(u, e3, split3)
        mid_res = mid_rhs[u] - active * product(mid_split, NPM, high, low)[:NP1]
        rhs = exact(rlow, mid_res)
        low_rhs[u] = rhs
        e4[u + SIDE] = rhs * (DAMPING * active / jac_of(u)) / diag_low

    over(SIDE, PAIRS - SIDE, mid_block)
    mid_right.wait_recv()
    for b in left_halo:
        split_mid(split3, b, e3[b])
    over_left(mid_block)
    low_left = send(3, e4, 1)
    mid_left.wait_recv()
    for b in right_halo:
        split_mid(split3, b, e3[b])
    over_right(mid_block)
    low_right = send(3, e4, 0)

    def members(u):
        rows = lax.broadcasted_iota(jnp.int32, (EC_DEV, PAIR), 0)
        return jnp.where(rows == row_of(agg_ref, 0, u), 1.0, 0.0).astype(BF16)

    coarse_sum[...] = jnp.zeros_like(coarse_sum)

    def low_block(u):
        active = active_of(u)
        high, low = low_feed(u, e4)
        low_res = low_rhs[u] - active * product(low_split, NPL, high, low)[:NP2]
        both = lax.dot_general(
            jnp.concatenate(parts(below(low_res, NPL - NP2)), axis=0),
            members(u),
            NT,
            preferred_element_type=F32,
        )
        coarse_sum[...] += both[:NP2] + both[NPL : NPL + NP2]

    over(SIDE, PAIRS - SIDE, low_block)
    low_left.wait_recv()
    over_right(low_block)
    low_right.wait_recv()
    over_left(low_block)

    def smoothed_away(value):
        return value - DAMPING * exact(stiff_low, value / diag_low)

    coarse = coarse_sum[...]
    residue = smoothed_away(coarse)
    swap_out[...] = residue
    swaps = [
        pltpu.make_async_remote_copy(
            src_ref=swap_out,
            dst_ref=swap_in.at[i],
            send_sem=swap_send.at[i],
            recv_sem=swap_recv.at[i],
            device_id={"fold": other},
            device_id_type=MESH,
        )
        for i, other in enumerate(partners)
    ]
    for swap in swaps:
        swap.start()
    for swap in swaps:
        swap.wait_recv()
    pair_sum = residue + swap_in[0]
    top = smoothed_away(pair_sum + (swap_in[1] + swap_in[2]))
    corr = (DAMPING / AGG) * (coarse + 0.5 * pair_sum + 0.25 * top) / diag_low
    corr_split = jnp.concatenate(parts(below(corr, NPL - NP2)), axis=0)

    def ascend_block(u):
        active = active_of(u)
        both = jnp.dot(corr_split, members(u), preferred_element_type=F32)
        low_total = e4[u + SIDE] + active * (both[:NP2] + both[NPL : NPL + NP2])
        high, low = parts(below(low_total, NPL - NP2))
        up = jnp.dot(rlow_t, high, preferred_element_type=F32)
        up = up[:NP1] + up[NP1:] + jnp.dot(rlow_t[:NP1], low, preferred_element_type=F32)
        total = e3[u + SIDE] + up
        e5[u + SIDE] = total
        split_mid(split5, u + SIDE, total)

    def update_block(u):
        high, low = split5[u + SIDE, pl.ds(0, NPM), :], split5[u + SIDE, pl.ds(NPM, NPM), :]
        put_wide(upd_ref, u, e2[u + SIDE] + product(rmid_t_split, NP0, high, low))

    def ascend_both(u):
        ascend_block(u)
        update_block(u)

    over_left(ascend_block)
    last_left = send(4, e5, 1)
    over_right(ascend_block)
    last_right = send(4, e5, 0)
    over(SIDE, PAIRS - SIDE, ascend_both)
    over_left(update_block)
    over_right(update_block)

    def residual_block(u):
        high, low = mid_feed(u, e5, split5)
        put_wide(res_ref, u, second[u] - active_of(u) * product(lift_split, NP0, high, low))

    over(SIDE, PAIRS - SIDE, residual_block)
    last_left.wait_recv()
    for b in right_halo:
        split_mid(split5, b, e5[b])
    over_right(residual_block)
    last_right.wait_recv()
    for b in left_halo:
        split_mid(split5, b, e5[b])
    over_left(residual_block)
    for copy in (*pending, *swaps):
        copy.wait_send()


def on_device(
    n_dom,
    n_fold,
    iterate,
    right_side,
    jacobian,
    face_scale,
    face_offset,
    agglomerate,
    live_count,
    stiff_fine,
    flux_fine,
    smoother,
    restrict_mid,
    restrict_low,
):
    def flat(array):
        return held(array.reshape(-1, LANES))

    def held(array):
        return pltpu.with_memory_space_constraint(array, pltpu.HBM)

    vmem = pl.BlockSpec(memory_space=pltpu.VMEM)
    hbm = pl.BlockSpec(memory_space=pltpu.HBM)
    smem = pl.BlockSpec(memory_space=pltpu.SMEM)
    out = jax.ShapeDtypeStruct((NP0 * ROWS_PER, LANES), F32)
    updated, residual = pl.pallas_call(
        partial(kernel, n_dom, n_fold),
        out_shape=(out, out),
        in_specs=[hbm] * 6 + [smem] + [hbm] * 5,
        out_specs=(vmem, vmem),
        scratch_shapes=[
            pltpu.VMEM((NP0 * ROWS_PER, LANES), F32),
            pltpu.VMEM((NP0 * ROWS_PER, LANES), F32),
            pltpu.VMEM((ROWS_PER, LANES), F32),
            pltpu.VMEM((FACES * ROWS_PER, LANES), F32),
            pltpu.VMEM((FACES * ROWS_PER, LANES), jnp.int32),
            pltpu.VMEM((ROWS_PER, LANES), jnp.int32),
            pltpu.VMEM((NP0, NP0), F32),
            pltpu.VMEM((FACES, NP0, NP0), F32),
            pltpu.VMEM((NP0, NP0), F32),
            pltpu.VMEM((NP1, NP0), F32),
            pltpu.VMEM((NP2, NP1), F32),
            pltpu.VMEM((EXT, NP0, PAIR), F32),
            pltpu.VMEM((EXT, NP0, PAIR), F32),
            pltpu.VMEM((EXT, NP1, PAIR), F32),
            pltpu.VMEM((EXT, NP2, PAIR), F32),
            pltpu.VMEM((EXT, NP1, PAIR), F32),
            pltpu.VMEM((EXT, 2 * MX_ROWS, PAIR), BF16),
            pltpu.VMEM((EXT, 2 * MX_ROWS, PAIR), BF16),
            pltpu.VMEM((PAIRS, FACES, SPAN * PAIR, PAIR), BF16),
            pltpu.VMEM((PAIRS, NP0, PAIR), F32),
            pltpu.VMEM((EXT, 2 * NPM, PAIR), BF16),
            pltpu.VMEM((EXT, 2 * NPM, PAIR), BF16),
            pltpu.VMEM((PAIRS, NP1, PAIR), F32),
            pltpu.VMEM((PAIRS, NP2, PAIR), F32),
            pltpu.VMEM((NP2, EC_DEV), F32),
            pltpu.VMEM((KF, PAIR), BF16),
            pltpu.VMEM((KF, PAIR), BF16),
            pltpu.VMEM((2, KM, PAIR), BF16),
            pltpu.VMEM((2, KL, PAIR), BF16),
            pltpu.VMEM((NP0, KF), F32),
            pltpu.VMEM((2 * NP0, KF), BF16),
            pltpu.VMEM((2 * NP0, NP0), BF16),
            pltpu.VMEM((2 * NPM, NP0), BF16),
            pltpu.VMEM((2 * NPL, NP0), BF16),
            pltpu.VMEM((2 * NPM, KM), BF16),
            pltpu.VMEM((NP0, KM), F32),
            pltpu.VMEM((2 * NP0, KM), BF16),
            pltpu.VMEM((2 * NPL, KL), BF16),
            pltpu.VMEM((2 * NP0, NPM), BF16),
            pltpu.VMEM((NP0, KL), F32),
            pltpu.VMEM((NP2, EC_DEV), F32),
            pltpu.VMEM((3, NP2, EC_DEV), F32),
            pltpu.SemaphoreType.DMA((5, 2)),
            pltpu.SemaphoreType.DMA((5, 2)),
            pltpu.SemaphoreType.DMA((3,)),
            pltpu.SemaphoreType.DMA((3,)),
            pltpu.SemaphoreType.DMA((11,)),
        ],
        compiler_params=pltpu.CompilerParams(
            collective_id=0, has_side_effects=True, vmem_limit_bytes=44 * 1024 * 1024
        ),
    )(
        flat(iterate),
        flat(right_side),
        flat(jacobian),
        flat(face_scale),
        flat(face_offset),
        flat(agglomerate),
        live_count,
        held(stiff_fine),
        held(flux_fine),
        held(smoother),
        held(restrict_mid),
        held(restrict_low),
    )
    return updated.reshape(iterate.shape), residual.reshape(iterate.shape)


def solution(mesh):
    return jax.shard_map(
        partial(on_device, mesh.shape["dom"], mesh.shape["fold"]),
        mesh=mesh,
        in_specs=(
            P(None, "fold", "dom"),
            P(None, "fold", "dom"),
            P("fold", "dom"),
            P(None, "fold", "dom"),
            P(None, "fold", "dom"),
            P("fold", "dom"),
            P("fold", "dom"),
            P(),
            P(),
            P(),
            P(),
            P(),
        ),
        out_specs=(P(None, "fold", "dom"), P(None, "fold", "dom")),
        check_vma=False,
    )
```

```python
from functools import partial

import jax
import jax.numpy as jnp
from jax import lax
from jax.experimental import pallas as pl
from jax.experimental.pallas import tpu as pltpu
from jax.sharding import PartitionSpec as P

NP0, NP1, NP2 = 176, 56, 24
FACES = 4
AGG = 8
HLEV = 2
HALO = 512
EC_DEV = 256
E_DEV = 2048
LANES = 128
PAIR = 256
PAIRS = E_DEV // PAIR
SIDE = HALO // PAIR
SPAN = 2 * SIDE + 1
EXT = PAIRS + 2 * SIDE
ROWS_PER = E_DEV // LANES
DAMPING = 0.8
NPM = 64
NPL = 32
KF = 896
KM = 5 * NPM
KL = 5 * NPL
MX_ROWS = 112
MX_FACES = 2
MESH = pl.DeviceIdType.MESH
F32, BF16 = jnp.float32, jnp.bfloat16
NN = (((1,), (0,)), ((), ()))
NT = (((1,), (1,)), ((), ()))


def exact(a, b, dims=NN):
    return lax.dot_general(a, b, dims, precision=lax.Precision.HIGHEST, preferred_element_type=F32)


def parts(x):
    high = x.astype(BF16)
    low = (x - high.astype(F32)).astype(BF16)
    return high, low


def store_parts(ref, x, rows):
    high, low = parts(x)
    ref[pl.ds(0, x.shape[0]), :] = high
    ref[pl.ds(rows, x.shape[0]), :] = low


def product(split_ref, rows, high, low):
    both = jnp.dot(split_ref[...], high, preferred_element_type=F32)
    rest = jnp.dot(split_ref[pl.ds(0, rows), :], low, preferred_element_type=F32)
    return both[:rows] + both[rows:] + rest


def kernel(
    n_dom,
    n_fold,
    iter_hbm,
    rhs_hbm,
    jac_hbm,
    scale_hbm,
    offset_hbm,
    agg_hbm,
    live_ref,
    stiff_hbm,
    flux_hbm,
    smoother_hbm,
    rmid_hbm,
    rlow_hbm,
    upd_ref,
    res_ref,
    iter_ref,
    rhs_ref,
    jac_ref,
    scale_ref,
    offset_ref,
    agg_ref,
    stiff_ref,
    flux_ref,
    smoother_ref,
    rmid_ref,
    rlow_ref,
    e1,
    e2,
    e3,
    e4,
    e5,
    split1,
    split2,
    pick,
    second,
    split3,
    split5,
    mid_rhs,
    low_rhs,
    coarse_sum,
    feed_high,
    feed_low,
    feed_mid,
    feed_coarse,
    fine_f32,
    fine_split,
    smooth_split,
    rmid_split,
    rboth_split,
    mid_split,
    lift_f32,
    lift_split,
    low_split,
    rmid_t_split,
    rlow_split,
    low_t_f32,
    swap_out,
    swap_in,
    send_sem,
    recv_sem,
    swap_send,
    swap_recv,
    load_sem,
):
    me = lax.axis_index("dom")
    fold = lax.axis_index("fold")
    right = lax.rem(me + 1, n_dom)
    left = lax.rem(me + n_dom - 1, n_dom)
    low_bit, high_bit = fold % 2, (fold // 2) % 2
    flip = fold + 1 - 2 * low_bit
    across = 2 - 4 * high_bit
    partners = (flip, fold + across, flip + across)

    loads = [
        pltpu.make_async_copy(source, target, load_sem.at[i])
        for i, (source, target) in enumerate(
            (
                (iter_hbm, iter_ref),
                (offset_hbm, offset_ref),
                (flux_hbm, flux_ref),
                (stiff_hbm, stiff_ref),
                (smoother_hbm, smoother_ref),
                (scale_hbm, scale_ref),
                (jac_hbm, jac_ref),
                (rhs_hbm, rhs_ref),
                (rmid_hbm, rmid_ref),
                (rlow_hbm, rlow_ref),
                (agg_hbm, agg_ref),
            )
        )
    ]
    for load in loads:
        load.start()

    barrier = pltpu.get_barrier_semaphore()
    for other in (left, right):
        pl.semaphore_signal(barrier, inc=1, device_id={"dom": other}, device_id_type=MESH)
    for other in partners:
        pl.semaphore_signal(barrier, inc=1, device_id={"fold": other}, device_id_type=MESH)

    lane = lax.broadcasted_iota(jnp.int32, (1, PAIR), 1)
    live = live_ref[0, 0]

    def row_of(ref, base, u):
        return jnp.concatenate(
            [ref[pl.ds(base + 2 * u, 1), :], ref[pl.ds(base + 2 * u + 1, 1), :]], axis=1
        )

    def active_of(u):
        return jnp.where(u * PAIR + lane < live, 1.0, 0.0).astype(F32)

    def jac_of(u):
        return row_of(jac_ref, 0, u)

    def weight_of(f, u):
        offset = row_of(offset_ref, f * ROWS_PER, u)
        target = me * E_DEV + u * PAIR + lane + offset
        inside = (offset != 0) & (target >= 0) & (target < n_dom * E_DEV)
        return jnp.where(inside, row_of(scale_ref, f * ROWS_PER, u), 0.0)

    def wide(ref, u):
        return jnp.concatenate(
            [ref[pl.ds(2 * u + h, NP0, stride=ROWS_PER), :] for h in range(2)], axis=1
        )

    def put_wide(ref, u, value):
        for h in range(2):
            ref[pl.ds(2 * u + h, NP0, stride=ROWS_PER), :] = value[:, h * LANES : (h + 1) * LANES]

    pending = []

    def send(k, buffer, side):
        copy = pltpu.make_async_remote_copy(
            src_ref=buffer.at[pl.ds(PAIRS if side == 0 else SIDE, SIDE)],
            dst_ref=buffer.at[pl.ds(0 if side == 0 else SIDE + PAIRS, SIDE)],
            send_sem=send_sem.at[k, side],
            recv_sem=recv_sem.at[k, side],
            device_id={"dom": right if side == 0 else left},
            device_id_type=MESH,
        )
        copy.start()
        pending.append(copy)
        return copy

    def over(first, last, body):
        def both(i, carry):
            body(first + 2 * i, 0)
            body(first + 2 * i + 1, 1)
            return carry

        lax.fori_loop(0, (last - first) // 2, both, 0)

    def over_one(first, last, body):
        def one(i, carry):
            body(i, 0)
            return carry

        lax.fori_loop(first, last, one, 0)

    def over_left(body):
        over(0, SIDE, body)

    def over_right(body):
        over(PAIRS - SIDE, PAIRS, body)

    def mask_block(u, slot):
        e1[u + SIDE] = active_of(u) * wide(iter_ref, u)

    loads[0].wait()
    over_left(mask_block)
    over_right(mask_block)
    pl.semaphore_wait(barrier, 2 + len(partners))
    from_left = send(0, e1, 0)
    from_right = send(0, e1, 1)
    over(SIDE, PAIRS - SIDE, mask_block)
    for load in loads[1:]:
        load.wait()

    def split_block(source, target, b):
        store_parts(target.at[b], source[b, pl.ds(0, MX_ROWS), :], MX_ROWS)

    def split_mid(target, b, value):
        padded = jnp.concatenate([value, jnp.zeros((NPM - NP1, PAIR), F32)], axis=0)
        store_parts(target.at[b], padded, NPM)

    left_halo = tuple(range(SIDE))
    right_halo = tuple(range(SIDE + PAIRS, EXT))

    over(SIDE, SIDE + PAIRS, lambda b, slot: split_block(e1, split1, b))

    fine_f32[...] = jnp.zeros_like(fine_f32)
    for f in range(FACES):
        fine_f32[:, f * NP0 : (f + 1) * NP0] = flux_ref[f]
    fine_f32[:, FACES * NP0 : (FACES + 1) * NP0] = stiff_ref[...]
    store_parts(fine_split, fine_f32[...], NP0)
    store_parts(smooth_split, smoother_ref[...], NP0)
    feed_high[...] = jnp.zeros_like(feed_high)
    feed_low[...] = jnp.zeros_like(feed_low)

    def build_pick(u, f):
        reach = lane + row_of(offset_ref, f * ROWS_PER, u) + HALO
        rows = lax.broadcasted_iota(jnp.int32, (PAIR, PAIR), 0)
        for j in range(SPAN):
            pick[u, f, pl.ds(j * PAIR, PAIR), :] = jnp.where(
                rows + j * PAIR == reach, 1.0, 0.0
            ).astype(BF16)

    reach_lane = lax.broadcasted_iota(jnp.int32, (8, LANES), 1)

    def lane_gather(u, buffer, f, first, rows, padding=0):
        halves = []
        for h in range(2):
            offset = offset_ref[pl.ds(f * ROWS_PER + 2 * u + h, 1), :]
            reach = jnp.broadcast_to(offset, (8, LANES)) + reach_lane + HALO
            inner = reach & (LANES - 1)
            outer = reach >> 7
            groups = []
            for g in range(rows // 8):
                value = None
                for j in range(2 * HALO // LANES + 1):
                    b = h + j
                    source = buffer[
                        u + b // 2, pl.ds(first + 8 * g, 8), pl.ds((b % 2) * LANES, LANES)
                    ]
                    found = jnp.take_along_axis(source, inner, axis=1)
                    value = found if j == 0 else jnp.where(outer == j, found, value)
                groups.append(value)
            if padding:
                groups.append(jnp.zeros((padding, LANES), F32))
            halves.append(jnp.concatenate(groups, axis=0))
        return jnp.concatenate(halves, axis=1)

    def fine_apply(u, slot, source, split, build):
        around = jnp.concatenate([split[u + j] for j in range(SPAN)], axis=1)
        for f in range(FACES):
            if build:
                build_pick(u, f)
            weight = weight_of(f, u)
            both = jnp.dot(around, pick[u, f], preferred_element_type=F32)
            high, low = parts((both[:MX_ROWS] + both[MX_ROWS:]) * weight)
            feed_high[slot, pl.ds(f * NP0, MX_ROWS), :] = high
            feed_low[slot, pl.ds(f * NP0, MX_ROWS), :] = low
            rest = lane_gather(u, source, f, MX_ROWS, NP0 - MX_ROWS)
            high, low = parts(rest * weight)
            feed_high[slot, pl.ds(f * NP0 + MX_ROWS, NP0 - MX_ROWS), :] = high
            feed_low[slot, pl.ds(f * NP0 + MX_ROWS, NP0 - MX_ROWS), :] = low
        high, low = parts(jac_of(u) * source[u + SIDE])
        feed_high[slot, pl.ds(FACES * NP0, NP0), :] = high
        feed_low[slot, pl.ds(FACES * NP0, NP0), :] = low
        return product(fine_split, NP0, feed_high[slot], feed_low[slot])

    def smooth_block(u, slot):
        active = active_of(u)
        first_res = active * (wide(rhs_ref, u) - fine_apply(u, slot, e1, split1, True))
        high, low = parts(first_res)
        update = product(smooth_split, NP0, high, low)
        block = e1[u + SIDE] + update * (active / jac_of(u))
        e2[u + SIDE] = block
        store_parts(split2.at[u + SIDE], block[:MX_ROWS], MX_ROWS)

    over_one(SIDE, PAIRS - SIDE, smooth_block)

    rmid = rmid_ref[...]
    rlow = rlow_ref[...]
    rboth = exact(rlow, rmid)
    lift_f32[...] = jnp.zeros_like(lift_f32)
    low_t_f32[...] = jnp.zeros_like(low_t_f32)
    rmid_t_split[...] = jnp.zeros_like(rmid_t_split)

    def identity(n):
        rows = lax.broadcasted_iota(jnp.int32, (n, n), 0)
        cols = lax.broadcasted_iota(jnp.int32, (n, n), 1)
        return jnp.where(rows == cols, 1.0, 0.0).astype(F32)

    def below(value, rows):
        return jnp.concatenate([value, jnp.zeros((rows, value.shape[1]), F32)], axis=0)

    def turned(value):
        unit = identity(value.shape[1]).astype(BF16)
        return [
            lax.dot_general(unit, part, NT, preferred_element_type=F32).astype(BF16)
            for part in parts(value)
        ]

    store_parts(rmid_split, below(rmid, NPM - NP1), NPM)
    store_parts(rboth_split, below(rboth, NPL - NP2), NPL)
    stacked = jnp.concatenate([below(rmid, NPM - NP1), below(rboth, NPL - NP2)], axis=0)
    stacked_high, stacked_low = turned(stacked)
    for f in range(FACES + 1):
        high, low = parts(flux_ref[f] if f < FACES else stiff_ref[...])
        lifted = (
            jnp.dot(high, stacked_high, preferred_element_type=F32)
            + jnp.dot(low, stacked_high, preferred_element_type=F32)
            + jnp.dot(high, stacked_low, preferred_element_type=F32)
        )
        lift_f32[:, f * NPM : (f + 1) * NPM] = lifted[:, :NPM]
        low_t_f32[:, f * NPL : (f + 1) * NPL] = lifted[:, NPM : NPM + NPL]
    lift = lift_f32[...]
    store_parts(lift_split, lift, NP0)
    mid_matrix = product(rmid_split, NPM, *parts(lift))
    low_matrix = product(rboth_split, NPL, *parts(low_t_f32[...]))
    store_parts(mid_split, mid_matrix, NPM)
    store_parts(low_split, low_matrix, NPL)
    mid_own = mid_matrix[:NP1, FACES * NPM : FACES * NPM + NP1]
    stiff_low = low_matrix[:NP2, FACES * NPL : FACES * NPL + NP2]
    diag_mid = jnp.sum(mid_own * identity(NP1), axis=1, keepdims=True)
    diag_low = jnp.sum(stiff_low * identity(NP2), axis=1, keepdims=True)
    rmid_t_split[pl.ds(0, NP0), :] = stacked_high[:, :NPM]
    rmid_t_split[pl.ds(NP0, NP0), :] = stacked_low[:, :NPM]
    rlow_wide = jnp.concatenate([rlow, jnp.zeros((NP2, NPM - NP1), F32)], axis=1)
    store_parts(rlow_split, below(rlow_wide, NPL - NP2), NPL)
    rlow_t_high, rlow_t_low = turned(below(rlow, NPL - NP2))
    rlow_t = jnp.concatenate([rlow_t_high, rlow_t_low], axis=0)

    from_left.wait_recv()
    for b in left_halo:
        split_block(e1, split1, b)
    over_one(0, SIDE, smooth_block)
    to_left = send(1, e2, 1)
    from_right.wait_recv()
    for b in right_halo:
        split_block(e1, split1, b)
    over_one(PAIRS - SIDE, PAIRS, smooth_block)
    to_right = send(1, e2, 0)

    def second_block(u, slot):
        active = active_of(u)
        block = active * (wide(rhs_ref, u) - fine_apply(u, slot, e2, split2, False))
        second[u] = block
        high, low = parts(block)
        rhs = product(rmid_split, NPM, high, low)[:NP1]
        mid_rhs[u] = rhs
        corr = rhs * (DAMPING * active / jac_of(u)) / diag_mid
        e3[u + SIDE] = corr
        split_mid(split3, u + SIDE, corr)

    over_one(SIDE, PAIRS - SIDE, second_block)
    to_left.wait_recv()
    for b in right_halo:
        split_block(e2, split2, b)
    over_one(PAIRS - SIDE, PAIRS, second_block)
    mid_right = send(2, e3, 0)
    to_right.wait_recv()
    for b in left_halo:
        split_block(e2, split2, b)
    over_one(0, SIDE, second_block)
    mid_left = send(2, e3, 1)

    def mid_feed(u, slot, buffer, split):
        around = jnp.concatenate([split[u + j] for j in range(SPAN)], axis=1)
        for f in range(FACES):
            if f < MX_FACES:
                both = jnp.dot(around, pick[u, f], preferred_element_type=F32)
                value = both[:NPM] + both[NPM:]
            else:
                value = lane_gather(u, buffer, f, 0, NP1, NPM - NP1)
            high, low = parts(value * weight_of(f, u))
            feed_mid[slot, 0, pl.ds(f * NPM, NPM), :] = high
            feed_mid[slot, 1, pl.ds(f * NPM, NPM), :] = low
        high, low = parts(below(jac_of(u) * buffer[u + SIDE], NPM - NP1))
        feed_mid[slot, 0, pl.ds(FACES * NPM, NPM), :] = high
        feed_mid[slot, 1, pl.ds(FACES * NPM, NPM), :] = low
        return feed_mid[slot, 0], feed_mid[slot, 1]

    def low_feed(u, slot, buffer):
        for f in range(FACES):
            value = lane_gather(u, buffer, f, 0, NP2, NPL - NP2)
            high, low = parts(value * weight_of(f, u))
            feed_coarse[slot, 0, pl.ds(f * NPL, NPL), :] = high
            feed_coarse[slot, 1, pl.ds(f * NPL, NPL), :] = low
        high, low = parts(below(jac_of(u) * buffer[u + SIDE], NPL - NP2))
        feed_coarse[slot, 0, pl.ds(FACES * NPL, NPL), :] = high
        feed_coarse[slot, 1, pl.ds(FACES * NPL, NPL), :] = low
        return feed_coarse[slot, 0], feed_coarse[slot, 1]

    def mid_block(u, slot):
        active = active_of(u)
        high, low = mid_feed(u, slot, e3, split3)
        mid_res = mid_rhs[u] - active * product(mid_split, NPM, high, low)[:NP1]
        high, low = parts(below(mid_res, NPM - NP1))
        rhs = product(rlow_split, NPL, high, low)[:NP2]
        low_rhs[u] = rhs
        e4[u + SIDE] = rhs * (DAMPING * active / jac_of(u)) / diag_low

    over(SIDE, PAIRS - SIDE, mid_block)
    mid_right.wait_recv()
    for b in left_halo:
        split_mid(split3, b, e3[b])
    over_left(mid_block)
    low_left = send(3, e4, 1)
    mid_left.wait_recv()
    for b in right_halo:
        split_mid(split3, b, e3[b])
    over_right(mid_block)
    low_right = send(3, e4, 0)

    def members(u):
        rows = lax.broadcasted_iota(jnp.int32, (EC_DEV, PAIR), 0)
        return jnp.where(rows == row_of(agg_ref, 0, u), 1.0, 0.0).astype(BF16)

    coarse_sum[...] = jnp.zeros_like(coarse_sum)

    def low_block(u, slot):
        active = active_of(u)
        high, low = low_feed(u, slot, e4)
        low_res = low_rhs[u] - active * product(low_split, NPL, high, low)[:NP2]
        both = lax.dot_general(
            jnp.concatenate(parts(below(low_res, NPL - NP2)), axis=0),
            members(u),
            NT,
            preferred_element_type=F32,
        )
        coarse_sum[...] += both[:NP2] + both[NPL : NPL + NP2]

    over(SIDE, PAIRS - SIDE, low_block)
    low_left.wait_recv()
    over_right(low_block)
    low_right.wait_recv()
    over_left(low_block)

    def smoothed_away(value):
        return value - DAMPING * exact(stiff_low, value / diag_low)

    coarse = coarse_sum[...]
    residue = smoothed_away(coarse)
    swap_out[...] = residue
    swaps = [
        pltpu.make_async_remote_copy(
            src_ref=swap_out,
            dst_ref=swap_in.at[i],
            send_sem=swap_send.at[i],
            recv_sem=swap_recv.at[i],
            device_id={"fold": other},
            device_id_type=MESH,
        )
        for i, other in enumerate(partners)
    ]
    for swap in swaps:
        swap.start()
    for swap in swaps:
        swap.wait_recv()
    pair_sum = residue + swap_in[0]
    top = smoothed_away(pair_sum + (swap_in[1] + swap_in[2]))
    corr = (DAMPING / AGG) * (coarse + 0.5 * pair_sum + 0.25 * top) / diag_low
    corr_split = jnp.concatenate(parts(below(corr, NPL - NP2)), axis=0)

    def ascend_block(u, slot):
        active = active_of(u)
        both = jnp.dot(corr_split, members(u), preferred_element_type=F32)
        low_total = e4[u + SIDE] + active * (both[:NP2] + both[NPL : NPL + NP2])
        high, low = parts(below(low_total, NPL - NP2))
        up = jnp.dot(rlow_t, high, preferred_element_type=F32)
        up = up[:NP1] + up[NP1:] + jnp.dot(rlow_t[:NP1], low, preferred_element_type=F32)
        total = e3[u + SIDE] + up
        e5[u + SIDE] = total
        split_mid(split5, u + SIDE, total)

    def update_block(u, slot):
        high, low = split5[u + SIDE, pl.ds(0, NPM), :], split5[u + SIDE, pl.ds(NPM, NPM), :]
        put_wide(upd_ref, u, e2[u + SIDE] + product(rmid_t_split, NP0, high, low))

    def ascend_both(u, slot):
        ascend_block(u, slot)
        update_block(u, slot)

    over_left(ascend_block)
    last_left = send(4, e5, 1)
    over_right(ascend_block)
    last_right = send(4, e5, 0)
    over(SIDE, PAIRS - SIDE, ascend_both)
    over_left(update_block)
    over_right(update_block)

    def residual_block(u, slot):
        high, low = mid_feed(u, slot, e5, split5)
        put_wide(res_ref, u, second[u] - active_of(u) * product(lift_split, NP0, high, low))

    over(SIDE, PAIRS - SIDE, residual_block)
    last_left.wait_recv()
    for b in right_halo:
        split_mid(split5, b, e5[b])
    over_right(residual_block)
    last_right.wait_recv()
    for b in left_halo:
        split_mid(split5, b, e5[b])
    over_left(residual_block)
    for copy in (*pending, *swaps):
        copy.wait_send()


def on_device(
    n_dom,
    n_fold,
    iterate,
    right_side,
    jacobian,
    face_scale,
    face_offset,
    agglomerate,
    live_count,
    stiff_fine,
    flux_fine,
    smoother,
    restrict_mid,
    restrict_low,
):
    def flat(array):
        return held(array.reshape(-1, LANES))

    def held(array):
        return pltpu.with_memory_space_constraint(array, pltpu.HBM)

    vmem = pl.BlockSpec(memory_space=pltpu.VMEM)
    hbm = pl.BlockSpec(memory_space=pltpu.HBM)
    smem = pl.BlockSpec(memory_space=pltpu.SMEM)
    out = jax.ShapeDtypeStruct((NP0 * ROWS_PER, LANES), F32)
    updated, residual = pl.pallas_call(
        partial(kernel, n_dom, n_fold),
        out_shape=(out, out),
        in_specs=[hbm] * 6 + [smem] + [hbm] * 5,
        out_specs=(vmem, vmem),
        scratch_shapes=[
            pltpu.VMEM((NP0 * ROWS_PER, LANES), F32),
            pltpu.VMEM((NP0 * ROWS_PER, LANES), F32),
            pltpu.VMEM((ROWS_PER, LANES), F32),
            pltpu.VMEM((FACES * ROWS_PER, LANES), F32),
            pltpu.VMEM((FACES * ROWS_PER, LANES), jnp.int32),
            pltpu.VMEM((ROWS_PER, LANES), jnp.int32),
            pltpu.VMEM((NP0, NP0), F32),
            pltpu.VMEM((FACES, NP0, NP0), F32),
            pltpu.VMEM((NP0, NP0), F32),
            pltpu.VMEM((NP1, NP0), F32),
            pltpu.VMEM((NP2, NP1), F32),
            pltpu.VMEM((EXT, NP0, PAIR), F32),
            pltpu.VMEM((EXT, NP0, PAIR), F32),
            pltpu.VMEM((EXT, NP1, PAIR), F32),
            pltpu.VMEM((EXT, NP2, PAIR), F32),
            pltpu.VMEM((EXT, NP1, PAIR), F32),
            pltpu.VMEM((EXT, 2 * MX_ROWS, PAIR), BF16),
            pltpu.VMEM((EXT, 2 * MX_ROWS, PAIR), BF16),
            pltpu.VMEM((PAIRS, FACES, SPAN * PAIR, PAIR), BF16),
            pltpu.VMEM((PAIRS, NP0, PAIR), F32),
            pltpu.VMEM((EXT, 2 * NPM, PAIR), BF16),
            pltpu.VMEM((EXT, 2 * NPM, PAIR), BF16),
            pltpu.VMEM((PAIRS, NP1, PAIR), F32),
            pltpu.VMEM((PAIRS, NP2, PAIR), F32),
            pltpu.VMEM((NP2, EC_DEV), F32),
            pltpu.VMEM((2, KF, PAIR), BF16),
            pltpu.VMEM((2, KF, PAIR), BF16),
            pltpu.VMEM((2, 2, KM, PAIR), BF16),
            pltpu.VMEM((2, 2, KL, PAIR), BF16),
            pltpu.VMEM((NP0, KF), F32),
            pltpu.VMEM((2 * NP0, KF), BF16),
            pltpu.VMEM((2 * NP0, NP0), BF16),
            pltpu.VMEM((2 * NPM, NP0), BF16),
            pltpu.VMEM((2 * NPL, NP0), BF16),
            pltpu.VMEM((2 * NPM, KM), BF16),
            pltpu.VMEM((NP0, KM), F32),
            pltpu.VMEM((2 * NP0, KM), BF16),
            pltpu.VMEM((2 * NPL, KL), BF16),
            pltpu.VMEM((2 * NP0, NPM), BF16),
            pltpu.VMEM((2 * NPL, NPM), BF16),
            pltpu.VMEM((NP0, KL), F32),
            pltpu.VMEM((NP2, EC_DEV), F32),
            pltpu.VMEM((3, NP2, EC_DEV), F32),
            pltpu.SemaphoreType.DMA((5, 2)),
            pltpu.SemaphoreType.DMA((5, 2)),
            pltpu.SemaphoreType.DMA((3,)),
            pltpu.SemaphoreType.DMA((3,)),
            pltpu.SemaphoreType.DMA((11,)),
        ],
        compiler_params=pltpu.CompilerParams(
            collective_id=0, has_side_effects=True, vmem_limit_bytes=48 * 1024 * 1024
        ),
    )(
        flat(iterate),
        flat(right_side),
        flat(jacobian),
        flat(face_scale),
        flat(face_offset),
        flat(agglomerate),
        live_count,
        held(stiff_fine),
        held(flux_fine),
        held(smoother),
        held(restrict_mid),
        held(restrict_low),
    )
    return updated.reshape(iterate.shape), residual.reshape(iterate.shape)


def solution(mesh):
    return jax.shard_map(
        partial(on_device, mesh.shape["dom"], mesh.shape["fold"]),
        mesh=mesh,
        in_specs=(
            P(None, "fold", "dom"),
            P(None, "fold", "dom"),
            P("fold", "dom"),
            P(None, "fold", "dom"),
            P(None, "fold", "dom"),
            P("fold", "dom"),
            P("fold", "dom"),
            P(),
            P(),
            P(),
            P(),
            P(),
        ),
        out_specs=(P(None, "fold", "dom"), P(None, "fold", "dom")),
        check_vma=False,
    )
```

```python
from functools import partial

import jax
import jax.numpy as jnp
from jax import lax
from jax.experimental import pallas as pl
from jax.experimental.pallas import tpu as pltpu
from jax.sharding import PartitionSpec as P

NP0, NP1, NP2 = 176, 56, 24
FACES = 4
AGG = 8
HLEV = 2
HALO = 512
EC_DEV = 256
E_DEV = 2048
LANES = 128
PAIR = 256
PAIRS = E_DEV // PAIR
SIDE = HALO // PAIR
SPAN = 2 * SIDE + 1
EXT = PAIRS + 2 * SIDE
ROWS_PER = E_DEV // LANES
DAMPING = 0.8
NPM = 64
NPL = 32
KF = 896
KM = 5 * NPM
KL = 5 * NPL
MX_ROWS = 112
MX_FACES = 2
MESH = pl.DeviceIdType.MESH
F32, BF16 = jnp.float32, jnp.bfloat16
NN = (((1,), (0,)), ((), ()))
NT = (((1,), (1,)), ((), ()))


def exact(a, b, dims=NN):
    return lax.dot_general(a, b, dims, precision=lax.Precision.HIGHEST, preferred_element_type=F32)


def parts(x):
    high = x.astype(BF16)
    low = (x - high.astype(F32)).astype(BF16)
    return high, low


def store_parts(ref, x, rows):
    high, low = parts(x)
    ref[pl.ds(0, x.shape[0]), :] = high
    ref[pl.ds(rows, x.shape[0]), :] = low


def product(split_ref, rows, high, low):
    both = jnp.dot(split_ref[...], high, preferred_element_type=F32)
    rest = jnp.dot(split_ref[pl.ds(0, rows), :], low, preferred_element_type=F32)
    return both[:rows] + both[rows:] + rest


def kernel(
    n_dom,
    n_fold,
    iter_hbm,
    rhs_hbm,
    jac_hbm,
    scale_hbm,
    offset_hbm,
    agg_hbm,
    live_ref,
    stiff_hbm,
    flux_hbm,
    smoother_hbm,
    rmid_hbm,
    rlow_hbm,
    upd_ref,
    res_ref,
    iter_ref,
    rhs_ref,
    jac_ref,
    scale_ref,
    offset_ref,
    agg_ref,
    stiff_ref,
    flux_ref,
    smoother_ref,
    rmid_ref,
    rlow_ref,
    e1,
    e2,
    e3,
    e4,
    e5,
    split1,
    split2,
    pick,
    second,
    split3,
    split5,
    mid_rhs,
    low_rhs,
    coarse_sum,
    feed_high,
    feed_low,
    feed_mid,
    feed_coarse,
    fine_f32,
    fine_split,
    smooth_split,
    rmid_split,
    rboth_split,
    mid_split,
    lift_f32,
    lift_split,
    low_split,
    rmid_t_split,
    rlow_split,
    low_t_f32,
    swap_out,
    swap_in,
    send_sem,
    recv_sem,
    swap_send,
    swap_recv,
    load_sem,
):
    me = lax.axis_index("dom")
    fold = lax.axis_index("fold")
    right = lax.rem(me + 1, n_dom)
    left = lax.rem(me + n_dom - 1, n_dom)
    low_bit, high_bit = fold % 2, (fold // 2) % 2
    flip = fold + 1 - 2 * low_bit
    across = 2 - 4 * high_bit
    partners = (flip, fold + across, flip + across)

    loads = [
        pltpu.make_async_copy(source, target, load_sem.at[i])
        for i, (source, target) in enumerate(
            (
                (iter_hbm, iter_ref),
                (offset_hbm, offset_ref),
                (flux_hbm, flux_ref),
                (stiff_hbm, stiff_ref),
                (smoother_hbm, smoother_ref),
                (scale_hbm, scale_ref),
                (jac_hbm, jac_ref),
                (rhs_hbm, rhs_ref),
                (rmid_hbm, rmid_ref),
                (rlow_hbm, rlow_ref),
                (agg_hbm, agg_ref),
            )
        )
    ]
    loads[0].start()

    barrier = pltpu.get_barrier_semaphore()
    for other in (left, right):
        pl.semaphore_signal(barrier, inc=1, device_id={"dom": other}, device_id_type=MESH)
    for other in partners:
        pl.semaphore_signal(barrier, inc=1, device_id={"fold": other}, device_id_type=MESH)

    lane = lax.broadcasted_iota(jnp.int32, (1, PAIR), 1)
    live = live_ref[0, 0]

    def row_of(ref, base, u):
        return jnp.concatenate(
            [ref[pl.ds(base + 2 * u, 1), :], ref[pl.ds(base + 2 * u + 1, 1), :]], axis=1
        )

    def active_of(u):
        return jnp.where(u * PAIR + lane < live, 1.0, 0.0).astype(F32)

    def jac_of(u):
        return row_of(jac_ref, 0, u)

    def weight_of(f, u):
        offset = row_of(offset_ref, f * ROWS_PER, u)
        target = me * E_DEV + u * PAIR + lane + offset
        inside = (offset != 0) & (target >= 0) & (target < n_dom * E_DEV)
        return jnp.where(inside, row_of(scale_ref, f * ROWS_PER, u), 0.0)

    def wide(ref, u):
        return jnp.concatenate(
            [ref[pl.ds(2 * u + h, NP0, stride=ROWS_PER), :] for h in range(2)], axis=1
        )

    def put_wide(ref, u, value):
        for h in range(2):
            ref[pl.ds(2 * u + h, NP0, stride=ROWS_PER), :] = value[:, h * LANES : (h + 1) * LANES]

    pending = []

    def send(k, buffer, side):
        copy = pltpu.make_async_remote_copy(
            src_ref=buffer.at[pl.ds(PAIRS if side == 0 else SIDE, SIDE)],
            dst_ref=buffer.at[pl.ds(0 if side == 0 else SIDE + PAIRS, SIDE)],
            send_sem=send_sem.at[k, side],
            recv_sem=recv_sem.at[k, side],
            device_id={"dom": right if side == 0 else left},
            device_id_type=MESH,
        )
        copy.start()
        pending.append(copy)
        return copy

    def over(first, last, body):
        def both(i, carry):
            body(first + 2 * i, 0)
            body(first + 2 * i + 1, 1)
            return carry

        lax.fori_loop(0, (last - first) // 2, both, 0)

    def over_one(first, last, body):
        def one(i, carry):
            body(i, 0)
            return carry

        lax.fori_loop(first, last, one, 0)

    def over_left(body):
        over(0, SIDE, body)

    def over_right(body):
        over(PAIRS - SIDE, PAIRS, body)

    def mask_block(u, slot):
        e1[u + SIDE] = active_of(u) * wide(iter_ref, u)

    loads[0].wait()
    for load in loads[1:]:
        load.start()
    over_left(mask_block)
    over_right(mask_block)
    pl.semaphore_wait(barrier, 2 + len(partners))
    from_left = send(0, e1, 0)
    from_right = send(0, e1, 1)
    over(SIDE, PAIRS - SIDE, mask_block)
    for load in loads[1:]:
        load.wait()

    def split_block(source, target, b):
        store_parts(target.at[b], source[b, pl.ds(0, MX_ROWS), :], MX_ROWS)

    def split_mid(target, b, value):
        padded = jnp.concatenate([value, jnp.zeros((NPM - NP1, PAIR), F32)], axis=0)
        store_parts(target.at[b], padded, NPM)

    left_halo = tuple(range(SIDE))
    right_halo = tuple(range(SIDE + PAIRS, EXT))

    over(SIDE, SIDE + PAIRS, lambda b, slot: split_block(e1, split1, b))

    fine_f32[...] = jnp.zeros_like(fine_f32)
    for f in range(FACES):
        fine_f32[:, f * NP0 : (f + 1) * NP0] = flux_ref[f]
    fine_f32[:, FACES * NP0 : (FACES + 1) * NP0] = stiff_ref[...]
    store_parts(fine_split, fine_f32[...], NP0)
    store_parts(smooth_split, smoother_ref[...], NP0)
    feed_high[...] = jnp.zeros_like(feed_high)
    feed_low[...] = jnp.zeros_like(feed_low)

    def build_pick(u, f):
        reach = lane + row_of(offset_ref, f * ROWS_PER, u) + HALO
        rows = lax.broadcasted_iota(jnp.int32, (PAIR, PAIR), 0)
        for j in range(SPAN):
            pick[u, f, pl.ds(j * PAIR, PAIR), :] = jnp.where(
                rows + j * PAIR == reach, 1.0, 0.0
            ).astype(BF16)

    reach_lane = lax.broadcasted_iota(jnp.int32, (8, LANES), 1)

    def lane_gather(u, buffer, f, first, rows, padding=0):
        halves = []
        for h in range(2):
            offset = offset_ref[pl.ds(f * ROWS_PER + 2 * u + h, 1), :]
            reach = jnp.broadcast_to(offset, (8, LANES)) + reach_lane + HALO
            inner = reach & (LANES - 1)
            outer = reach >> 7
            groups = []
            for g in range(rows // 8):
                value = None
                for j in range(2 * HALO // LANES + 1):
                    b = h + j
                    source = buffer[
                        u + b // 2, pl.ds(first + 8 * g, 8), pl.ds((b % 2) * LANES, LANES)
                    ]
                    found = jnp.take_along_axis(source, inner, axis=1)
                    value = found if j == 0 else jnp.where(outer == j, found, value)
                groups.append(value)
            if padding:
                groups.append(jnp.zeros((padding, LANES), F32))
            halves.append(jnp.concatenate(groups, axis=0))
        return jnp.concatenate(halves, axis=1)

    def fine_apply(u, slot, source, split, build):
        around = jnp.concatenate([split[u + j] for j in range(SPAN)], axis=1)
        for f in range(FACES):
            if build:
                build_pick(u, f)
            weight = weight_of(f, u)
            both = jnp.dot(around, pick[u, f], preferred_element_type=F32)
            high, low = parts((both[:MX_ROWS] + both[MX_ROWS:]) * weight)
            feed_high[slot, pl.ds(f * NP0, MX_ROWS), :] = high
            feed_low[slot, pl.ds(f * NP0, MX_ROWS), :] = low
            rest = lane_gather(u, source, f, MX_ROWS, NP0 - MX_ROWS)
            high, low = parts(rest * weight)
            feed_high[slot, pl.ds(f * NP0 + MX_ROWS, NP0 - MX_ROWS), :] = high
            feed_low[slot, pl.ds(f * NP0 + MX_ROWS, NP0 - MX_ROWS), :] = low
        high, low = parts(jac_of(u) * source[u + SIDE])
        feed_high[slot, pl.ds(FACES * NP0, NP0), :] = high
        feed_low[slot, pl.ds(FACES * NP0, NP0), :] = low
        return product(fine_split, NP0, feed_high[slot], feed_low[slot])

    def smooth_block(u, slot):
        active = active_of(u)
        first_res = active * (wide(rhs_ref, u) - fine_apply(u, slot, e1, split1, True))
        high, low = parts(first_res)
        update = product(smooth_split, NP0, high, low)
        block = e1[u + SIDE] + update * (active / jac_of(u))
        e2[u + SIDE] = block
        store_parts(split2.at[u + SIDE], block[:MX_ROWS], MX_ROWS)

    over_one(SIDE, PAIRS - SIDE, smooth_block)

    rmid = rmid_ref[...]
    rlow = rlow_ref[...]
    rboth = exact(rlow, rmid)
    lift_f32[...] = jnp.zeros_like(lift_f32)
    low_t_f32[...] = jnp.zeros_like(low_t_f32)
    rmid_t_split[...] = jnp.zeros_like(rmid_t_split)

    def identity(n):
        rows = lax.broadcasted_iota(jnp.int32, (n, n), 0)
        cols = lax.broadcasted_iota(jnp.int32, (n, n), 1)
        return jnp.where(rows == cols, 1.0, 0.0).astype(F32)

    def below(value, rows):
        return jnp.concatenate([value, jnp.zeros((rows, value.shape[1]), F32)], axis=0)

    def turned(value):
        unit = identity(value.shape[1]).astype(BF16)
        return [
            lax.dot_general(unit, part, NT, preferred_element_type=F32).astype(BF16)
            for part in parts(value)
        ]

    store_parts(rmid_split, below(rmid, NPM - NP1), NPM)
    store_parts(rboth_split, below(rboth, NPL - NP2), NPL)
    stacked = jnp.concatenate([below(rmid, NPM - NP1), below(rboth, NPL - NP2)], axis=0)
    stacked_high, stacked_low = turned(stacked)
    for f in range(FACES + 1):
        high, low = parts(flux_ref[f] if f < FACES else stiff_ref[...])
        lifted = (
            jnp.dot(high, stacked_high, preferred_element_type=F32)
            + jnp.dot(low, stacked_high, preferred_element_type=F32)
            + jnp.dot(high, stacked_low, preferred_element_type=F32)
        )
        lift_f32[:, f * NPM : (f + 1) * NPM] = lifted[:, :NPM]
        low_t_f32[:, f * NPL : (f + 1) * NPL] = lifted[:, NPM : NPM + NPL]
    lift = lift_f32[...]
    store_parts(lift_split, lift, NP0)
    mid_matrix = product(rmid_split, NPM, *parts(lift))
    low_matrix = product(rboth_split, NPL, *parts(low_t_f32[...]))
    store_parts(mid_split, mid_matrix, NPM)
    store_parts(low_split, low_matrix, NPL)
    mid_own = mid_matrix[:NP1, FACES * NPM : FACES * NPM + NP1]
    stiff_low = low_matrix[:NP2, FACES * NPL : FACES * NPL + NP2]
    diag_mid = jnp.sum(mid_own * identity(NP1), axis=1, keepdims=True)
    diag_low = jnp.sum(stiff_low * identity(NP2), axis=1, keepdims=True)
    rmid_t_split[pl.ds(0, NP0), :] = stacked_high[:, :NPM]
    rmid_t_split[pl.ds(NP0, NP0), :] = stacked_low[:, :NPM]
    rlow_wide = jnp.concatenate([rlow, jnp.zeros((NP2, NPM - NP1), F32)], axis=1)
    store_parts(rlow_split, below(rlow_wide, NPL - NP2), NPL)
    rlow_t_high, rlow_t_low = turned(below(rlow, NPL - NP2))
    rlow_t = jnp.concatenate([rlow_t_high, rlow_t_low], axis=0)

    from_left.wait_recv()
    for b in left_halo:
        split_block(e1, split1, b)
    over_one(0, SIDE, smooth_block)
    to_left = send(1, e2, 1)
    from_right.wait_recv()
    for b in right_halo:
        split_block(e1, split1, b)
    over_one(PAIRS - SIDE, PAIRS, smooth_block)
    to_right = send(1, e2, 0)

    def second_block(u, slot):
        active = active_of(u)
        block = active * (wide(rhs_ref, u) - fine_apply(u, slot, e2, split2, False))
        second[u] = block
        high, low = parts(block)
        rhs = product(rmid_split, NPM, high, low)[:NP1]
        mid_rhs[u] = rhs
        corr = rhs * (DAMPING * active / jac_of(u)) / diag_mid
        e3[u + SIDE] = corr
        split_mid(split3, u + SIDE, corr)

    over_one(SIDE, PAIRS - SIDE, second_block)
    to_left.wait_recv()
    for b in right_halo:
        split_block(e2, split2, b)
    over_one(PAIRS - SIDE, PAIRS, second_block)
    mid_right = send(2, e3, 0)
    to_right.wait_recv()
    for b in left_halo:
        split_block(e2, split2, b)
    over_one(0, SIDE, second_block)
    mid_left = send(2, e3, 1)

    def mid_feed(u, slot, buffer, split):
        around = jnp.concatenate([split[u + j] for j in range(SPAN)], axis=1)
        for f in range(FACES):
            if f < MX_FACES:
                both = jnp.dot(around, pick[u, f], preferred_element_type=F32)
                value = both[:NPM] + both[NPM:]
            else:
                value = lane_gather(u, buffer, f, 0, NP1, NPM - NP1)
            high, low = parts(value * weight_of(f, u))
            feed_mid[slot, 0, pl.ds(f * NPM, NPM), :] = high
            feed_mid[slot, 1, pl.ds(f * NPM, NPM), :] = low
        high, low = parts(below(jac_of(u) * buffer[u + SIDE], NPM - NP1))
        feed_mid[slot, 0, pl.ds(FACES * NPM, NPM), :] = high
        feed_mid[slot, 1, pl.ds(FACES * NPM, NPM), :] = low
        return feed_mid[slot, 0], feed_mid[slot, 1]

    def low_feed(u, slot, buffer):
        for f in range(FACES):
            value = lane_gather(u, buffer, f, 0, NP2, NPL - NP2)
            high, low = parts(value * weight_of(f, u))
            feed_coarse[slot, 0, pl.ds(f * NPL, NPL), :] = high
            feed_coarse[slot, 1, pl.ds(f * NPL, NPL), :] = low
        high, low = parts(below(jac_of(u) * buffer[u + SIDE], NPL - NP2))
        feed_coarse[slot, 0, pl.ds(FACES * NPL, NPL), :] = high
        feed_coarse[slot, 1, pl.ds(FACES * NPL, NPL), :] = low
        return feed_coarse[slot, 0], feed_coarse[slot, 1]

    def mid_block(u, slot):
        active = active_of(u)
        high, low = mid_feed(u, slot, e3, split3)
        mid_res = mid_rhs[u] - active * product(mid_split, NPM, high, low)[:NP1]
        high, low = parts(below(mid_res, NPM - NP1))
        rhs = product(rlow_split, NPL, high, low)[:NP2]
        low_rhs[u] = rhs
        e4[u + SIDE] = rhs * (DAMPING * active / jac_of(u)) / diag_low

    over(SIDE, PAIRS - SIDE, mid_block)
    mid_right.wait_recv()
    for b in left_halo:
        split_mid(split3, b, e3[b])
    over_left(mid_block)
    low_left = send(3, e4, 1)
    mid_left.wait_recv()
    for b in right_halo:
        split_mid(split3, b, e3[b])
    over_right(mid_block)
    low_right = send(3, e4, 0)

    def members(u):
        rows = lax.broadcasted_iota(jnp.int32, (EC_DEV, PAIR), 0)
        return jnp.where(rows == row_of(agg_ref, 0, u), 1.0, 0.0).astype(BF16)

    coarse_sum[...] = jnp.zeros_like(coarse_sum)

    def low_block(u, slot):
        active = active_of(u)
        high, low = low_feed(u, slot, e4)
        low_res = low_rhs[u] - active * product(low_split, NPL, high, low)[:NP2]
        both = lax.dot_general(
            jnp.concatenate(parts(below(low_res, NPL - NP2)), axis=0),
            members(u),
            NT,
            preferred_element_type=F32,
        )
        coarse_sum[...] += both[:NP2] + both[NPL : NPL + NP2]

    over(SIDE, PAIRS - SIDE, low_block)
    low_left.wait_recv()
    over_right(low_block)
    low_right.wait_recv()
    over_left(low_block)

    def smoothed_away(value):
        return value - DAMPING * exact(stiff_low, value / diag_low)

    coarse = coarse_sum[...]
    residue = smoothed_away(coarse)
    swap_out[...] = residue
    swaps = [
        pltpu.make_async_remote_copy(
            src_ref=swap_out,
            dst_ref=swap_in.at[i],
            send_sem=swap_send.at[i],
            recv_sem=swap_recv.at[i],
            device_id={"fold": other},
            device_id_type=MESH,
        )
        for i, other in enumerate(partners)
    ]
    for swap in swaps:
        swap.start()

    def up_from_low(value):
        high, low = parts(below(value, NPL - NP2))
        both = jnp.dot(rlow_t, high, preferred_element_type=F32)
        return both[:NP1] + both[NP1:] + jnp.dot(rlow_t[:NP1], low, preferred_element_type=F32)

    def own_block(u, slot):
        e5[u + SIDE] = e3[u + SIDE] + up_from_low(e4[u + SIDE])

    over(0, PAIRS, own_block)
    for swap in swaps:
        swap.wait_recv()
    pair_sum = residue + swap_in[0]
    top = smoothed_away(pair_sum + (swap_in[1] + swap_in[2]))
    corr = (DAMPING / AGG) * (coarse + 0.5 * pair_sum + 0.25 * top) / diag_low
    corr_split = jnp.concatenate(parts(below(up_from_low(corr), NPM - NP1)), axis=0)

    def ascend_block(u, slot):
        active = active_of(u)
        both = jnp.dot(corr_split, members(u), preferred_element_type=F32)
        total = e5[u + SIDE] + active * (both[:NP1] + both[NPM : NPM + NP1])
        e5[u + SIDE] = total
        split_mid(split5, u + SIDE, total)

    def update_block(u, slot):
        high, low = split5[u + SIDE, pl.ds(0, NPM), :], split5[u + SIDE, pl.ds(NPM, NPM), :]
        put_wide(upd_ref, u, e2[u + SIDE] + product(rmid_t_split, NP0, high, low))

    def ascend_both(u, slot):
        ascend_block(u, slot)
        update_block(u, slot)

    over_left(ascend_block)
    last_left = send(4, e5, 1)
    over_right(ascend_block)
    last_right = send(4, e5, 0)
    over(SIDE, PAIRS - SIDE, ascend_both)
    over_left(update_block)
    over_right(update_block)

    def residual_block(u, slot):
        high, low = mid_feed(u, slot, e5, split5)
        put_wide(res_ref, u, second[u] - active_of(u) * product(lift_split, NP0, high, low))

    over(SIDE, PAIRS - SIDE, residual_block)
    last_left.wait_recv()
    for b in right_halo:
        split_mid(split5, b, e5[b])
    over_right(residual_block)
    last_right.wait_recv()
    for b in left_halo:
        split_mid(split5, b, e5[b])
    over_left(residual_block)
    for copy in (*pending, *swaps):
        copy.wait_send()


def on_device(
    n_dom,
    n_fold,
    iterate,
    right_side,
    jacobian,
    face_scale,
    face_offset,
    agglomerate,
    live_count,
    stiff_fine,
    flux_fine,
    smoother,
    restrict_mid,
    restrict_low,
):
    def flat(array):
        return held(array.reshape(-1, LANES))

    def held(array):
        return pltpu.with_memory_space_constraint(array, pltpu.HBM)

    vmem = pl.BlockSpec(memory_space=pltpu.VMEM)
    hbm = pl.BlockSpec(memory_space=pltpu.HBM)
    smem = pl.BlockSpec(memory_space=pltpu.SMEM)
    out = jax.ShapeDtypeStruct((NP0 * ROWS_PER, LANES), F32)
    updated, residual = pl.pallas_call(
        partial(kernel, n_dom, n_fold),
        out_shape=(out, out),
        in_specs=[hbm] * 6 + [smem] + [hbm] * 5,
        out_specs=(vmem, vmem),
        scratch_shapes=[
            pltpu.VMEM((NP0 * ROWS_PER, LANES), F32),
            pltpu.VMEM((NP0 * ROWS_PER, LANES), F32),
            pltpu.VMEM((ROWS_PER, LANES), F32),
            pltpu.VMEM((FACES * ROWS_PER, LANES), F32),
            pltpu.VMEM((FACES * ROWS_PER, LANES), jnp.int32),
            pltpu.VMEM((ROWS_PER, LANES), jnp.int32),
            pltpu.VMEM((NP0, NP0), F32),
            pltpu.VMEM((FACES, NP0, NP0), F32),
            pltpu.VMEM((NP0, NP0), F32),
            pltpu.VMEM((NP1, NP0), F32),
            pltpu.VMEM((NP2, NP1), F32),
            pltpu.VMEM((EXT, NP0, PAIR), F32),
            pltpu.VMEM((EXT, NP0, PAIR), F32),
            pltpu.VMEM((EXT, NP1, PAIR), F32),
            pltpu.VMEM((EXT, NP2, PAIR), F32),
            pltpu.VMEM((EXT, NP1, PAIR), F32),
            pltpu.VMEM((EXT, 2 * MX_ROWS, PAIR), BF16),
            pltpu.VMEM((EXT, 2 * MX_ROWS, PAIR), BF16),
            pltpu.VMEM((PAIRS, FACES, SPAN * PAIR, PAIR), BF16),
            pltpu.VMEM((PAIRS, NP0, PAIR), F32),
            pltpu.VMEM((EXT, 2 * NPM, PAIR), BF16),
            pltpu.VMEM((EXT, 2 * NPM, PAIR), BF16),
            pltpu.VMEM((PAIRS, NP1, PAIR), F32),
            pltpu.VMEM((PAIRS, NP2, PAIR), F32),
            pltpu.VMEM((NP2, EC_DEV), F32),
            pltpu.VMEM((2, KF, PAIR), BF16),
            pltpu.VMEM((2, KF, PAIR), BF16),
            pltpu.VMEM((2, 2, KM, PAIR), BF16),
            pltpu.VMEM((2, 2, KL, PAIR), BF16),
            pltpu.VMEM((NP0, KF), F32),
            pltpu.VMEM((2 * NP0, KF), BF16),
            pltpu.VMEM((2 * NP0, NP0), BF16),
            pltpu.VMEM((2 * NPM, NP0), BF16),
            pltpu.VMEM((2 * NPL, NP0), BF16),
            pltpu.VMEM((2 * NPM, KM), BF16),
            pltpu.VMEM((NP0, KM), F32),
            pltpu.VMEM((2 * NP0, KM), BF16),
            pltpu.VMEM((2 * NPL, KL), BF16),
            pltpu.VMEM((2 * NP0, NPM), BF16),
            pltpu.VMEM((2 * NPL, NPM), BF16),
            pltpu.VMEM((NP0, KL), F32),
            pltpu.VMEM((NP2, EC_DEV), F32),
            pltpu.VMEM((3, NP2, EC_DEV), F32),
            pltpu.SemaphoreType.DMA((5, 2)),
            pltpu.SemaphoreType.DMA((5, 2)),
            pltpu.SemaphoreType.DMA((3,)),
            pltpu.SemaphoreType.DMA((3,)),
            pltpu.SemaphoreType.DMA((11,)),
        ],
        compiler_params=pltpu.CompilerParams(
            collective_id=0, has_side_effects=True, vmem_limit_bytes=48 * 1024 * 1024
        ),
    )(
        flat(iterate),
        flat(right_side),
        flat(jacobian),
        flat(face_scale),
        flat(face_offset),
        flat(agglomerate),
        live_count,
        held(stiff_fine),
        held(flux_fine),
        held(smoother),
        held(restrict_mid),
        held(restrict_low),
    )
    return updated.reshape(iterate.shape), residual.reshape(iterate.shape)


def solution(mesh):
    return jax.shard_map(
        partial(on_device, mesh.shape["dom"], mesh.shape["fold"]),
        mesh=mesh,
        in_specs=(
            P(None, "fold", "dom"),
            P(None, "fold", "dom"),
            P("fold", "dom"),
            P(None, "fold", "dom"),
            P(None, "fold", "dom"),
            P("fold", "dom"),
            P("fold", "dom"),
            P(),
            P(),
            P(),
            P(),
            P(),
        ),
        out_specs=(P(None, "fold", "dom"), P(None, "fold", "dom")),
        check_vma=False,
    )
```
